32 devices in a mesh: group: 2 (over y), clip: 4 (over x, core), seq: 4 (over z).
Axes of the slice: x: 2, y: 2, z: 4, core: 2. Of those that a mesh axis runs over, the one named last changes fastest.
Arguments:
- queries: bfloat16 [8, 512, 2048], P(('group', 'clip'), 'seq'), parts along dimension 0, may hold values from -18 to 18
- key_states: bfloat16 [8, 512, 2048], P(('group', 'clip'), 'seq'), parts along dimension 0, may hold values from -18 to 18
- value_states: bfloat16 [8, 512, 2048], P(('group', 'clip'), 'seq'), parts along dimension 0, may hold values from -6 to 6
- query_tangent: bfloat16 [8, 512, 2048], P(('group', 'clip'), 'seq'), parts along dimension 0, may hold values from -6 to 6
- key_tangent: bfloat16 [8, 512, 2048], P(('group', 'clip'), 'seq'), parts along dimension 0, may hold values from -6 to 6
- value_tangent: bfloat16 [8, 512, 2048], P(('group', 'clip'), 'seq'), parts along dimension 0, may hold values from -6 to 6
- offsets: int32 [8], P(('group', 'clip')), parts along dimension 0, may hold values from 0 to 130560
Outputs:
- attended: bfloat16 [8, 512, 2048], P(('group', 'clip'), 'seq'), parts along dimension 0
- attended_tangent: bfloat16 [8, 512, 2048], P(('group', 'clip'), 'seq'), parts along dimension 0
The draws below stay inside these ranges and needn't reach their ends.
There are 2 independent parts, one for each index of `group`. The reference program is written for one: setup_inputs(seed, part) draws one part's arguments, and reference() takes and returns one part's arrays. A program takes and returns all parts, laid end to end along the dimension named above; each array names one. Nothing has to cross between parts.
All inputs are finite; a program needn't handle non-finite values.
Results may differ from the reference program's by a relative error of at most 0.012.
The reference program's roundings to bfloat16 on the way (of `weights` and `product_half`) count: a program that leaves them out, or rounds other values in their place, can miss the bound.
Values may be sent and summed in bfloat16 or wider, within the bound.
No kernel may reach another device: no remote copies, remote signals or barrier semaphores. Data moves between devices by JAX's collectives and lax.ppermute only.
A program may use at most 64 MiB of HBM per device.

```python
import math
import jax
import jax.numpy as jnp
from jax import lax

H = 16
HD = 128
HH = 44
WW = 80
VIDEO = 131072
D = 2048
L = 512
CLIPS = 4


def paired_draw(key):
    base_q = jnp.clip(jax.random.normal(jax.random.fold_in(key, 101), (CLIPS, L, H, HD), jnp.float32), -6.0, 6.0)
    base_k = jnp.clip(jax.random.normal(jax.random.fold_in(key, 102), (CLIPS, L, H, HD), jnp.float32), -6.0, 6.0)
    return (base_q.reshape(CLIPS, L, H * HD), base_k.reshape(CLIPS, L, H * HD))


def draw_queries(key, part):
    return paired_draw(key)[0].astype(jnp.bfloat16)


def draw_key_states(key, part):
    return paired_draw(key)[1].astype(jnp.bfloat16)


def place_ends(values, rng, smallest, high):
    longest = values.shape.index(max(values.shape))
    spots = []
    for shift in (0, 1):
        where = [jax.random.randint(jax.random.fold_in(rng, axis), (), 0, length) for axis, length in enumerate(values.shape)]
        where[longest] = (where[longest] + shift) % values.shape[longest]
        spots.append(tuple(where))
    return values.at[spots[0]].set(smallest).at[spots[1]].set(high)


def shard_levels(own_key, dims, shards, smallest, high):
    level, own = 1.0, jax.random.fold_in(own_key, 6)
    for dim, blocks in shards:
        steps = jnp.exp(jax.random.uniform(jax.random.fold_in(own, dim), (blocks,), jnp.float32, smallest / len(shards), high / len(shards)))
        level = level * jnp.repeat(steps, dims[dim] // blocks).reshape([-1 if axis == dim else 1 for axis in range(len(dims))])
    return level


def centred(key, shape, deviation, limit, pieces=(), kind=jnp.bfloat16):
    factor_of = shard_levels(key, shape, pieces, -0.22, 0.18) if pieces else 1.0
    values = jax.random.normal(key, shape, jnp.float32) * deviation * factor_of
    return jnp.minimum(jnp.maximum(values, -limit), limit).astype(kind)


def setup_inputs(seed: int = 0, part: int = 0) -> dict:
    arg_keys = jax.random.split(jax.random.key(seed), 8)
    own_keys = jax.random.split(jax.random.fold_in(arg_keys[7], part), 8)
    return {
        "queries": draw_queries(jax.random.fold_in(jax.random.fold_in(arg_keys[7], part), 71), part),
        "key_states": draw_key_states(jax.random.fold_in(jax.random.fold_in(arg_keys[7], part), 71), part),
        "value_states": centred(own_keys[2], (CLIPS, L, D), 1.0, 6.0, ((0, 4), (1, 4))),
        "query_tangent": centred(own_keys[3], (CLIPS, L, D), 1.0, 6.0, ((0, 4), (1, 4))),
        "key_tangent": centred(own_keys[4], (CLIPS, L, D), 1.0, 6.0, ((0, 4), (1, 4))),
        "value_tangent": centred(own_keys[5], (CLIPS, L, D), 1.0, 6.0, ((0, 4), (1, 4))),
        "offsets": place_ends(jax.random.randint(own_keys[6], (CLIPS,), 0, VIDEO - L + 1), jax.random.fold_in(own_keys[6], 1), 0, VIDEO - L).astype(jnp.int32),
    }


rope_theta = 10000.0

def rope_tables(first, count):
    global_index = first + jnp.arange(count, dtype=jnp.int32)
    frames = global_index // (HH * WW)
    grid_row = global_index // WW % HH
    column = global_index % WW
    spatial = HD // 6 * 2
    temporal = HD - 2 * spatial
    channel = jnp.arange(HD, dtype=jnp.int32)
    part_start = jnp.where(channel < temporal, 0, jnp.where(channel < temporal + spatial, temporal, temporal + spatial))
    extent = jnp.where(channel < temporal, temporal, spatial)
    pair_index = (channel - part_start) // 2
    frequency = jnp.exp(-(2.0 * pair_index.astype(jnp.float32) / extent.astype(jnp.float32)) * math.log(rope_theta))
    position = jnp.where(channel[None, :] < temporal, frames[:, None], jnp.where(channel[None, :] < temporal + spatial, grid_row[:, None], column[:, None]))
    angles = position.astype(jnp.float32) * frequency[None, :]
    return (jnp.cos(angles)[:, None, :], jnp.sin(angles)[:, None, :])

def rotate(tensor, cosine, sine):
    channel = jnp.arange(tensor.shape[-1], dtype=jnp.int32)
    partner = jnp.where(channel % 2 == 0, -jnp.roll(tensor, -1, axis=-1), jnp.roll(tensor, 1, axis=-1))
    return (tensor * cosine + partner * sine).astype(jnp.bfloat16)

def attend_head(query_h, key_h, value_h, qdot_h, kdot_h, vdot_h):
    scaling = 1.0 / math.sqrt(HD)
    scores = jnp.dot(query_h, key_h.T, preferred_element_type=jnp.float32) * scaling
    probs = jax.nn.softmax(scores, axis=-1)
    weights = probs.astype(jnp.bfloat16)
    out_full = jnp.dot(weights, value_h, preferred_element_type=jnp.float32)
    scores_dot = (jnp.dot(qdot_h, key_h.T, preferred_element_type=jnp.float32) + jnp.dot(query_h, kdot_h.T, preferred_element_type=jnp.float32)) * scaling
    product = weights.astype(jnp.float32) * scores_dot
    correction = lax.optimization_barrier(jnp.sum(product, axis=-1, keepdims=True))
    product_half = product.astype(jnp.bfloat16)
    tangent = jnp.dot(weights, vdot_h, preferred_element_type=jnp.float32) + jnp.dot(product_half, value_h, preferred_element_type=jnp.float32) - correction * out_full
    return (out_full.astype(jnp.bfloat16), tangent.astype(jnp.bfloat16))

def reference(queries, key_states, value_states, query_tangent, key_tangent, value_tangent, offsets):

    def per_clip(inputs):
        query_in, key_in, value_in, qdot_in, kdot_in, vdot_in, start_at = inputs
        cosine, sine = rope_tables(start_at, L)

        def heads(array):
            return array.reshape(L, H, HD)
        rotated_q = rotate(heads(query_in).astype(jnp.float32), cosine, sine)
        rotated_k = rotate(heads(key_in).astype(jnp.float32), cosine, sine)
        rotated_qd = rotate(heads(qdot_in).astype(jnp.float32), cosine, sine)
        rotated_kd = rotate(heads(kdot_in).astype(jnp.float32), cosine, sine)
        stacked = tuple((jnp.transpose(array, (1, 0, 2)) for array in (rotated_q, rotated_k, heads(value_in), rotated_qd, rotated_kd, heads(vdot_in))))

        def per_head(parts):
            return attend_head(*parts)
        out_heads, tan_heads = lax.map(per_head, stacked)
        return (jnp.transpose(out_heads, (1, 0, 2)).reshape(L, H * HD), jnp.transpose(tan_heads, (1, 0, 2)).reshape(L, H * HD))
    attended, attended_tangent = lax.map(per_clip, (queries, key_states, value_states, query_tangent, key_tangent, value_tangent, offsets))
    return (attended, attended_tangent)
```

```python
import functools
import math

import jax
import jax.numpy as jnp
from jax import lax
from jax.experimental import pallas as pl
from jax.experimental.pallas import tpu as pltpu
from jax.sharding import PartitionSpec as P

H = 16
HD = 128
HH = 44
WW = 80


rope_theta = 10000.0


def rope_tables(first, count):
    global_index = first + jnp.arange(count, dtype=jnp.int32)
    frames = global_index // (HH * WW)
    grid_row = global_index // WW % HH
    column = global_index % WW
    spatial = HD // 6 * 2
    temporal = HD - 2 * spatial
    channel = jnp.arange(HD, dtype=jnp.int32)
    part_start = jnp.where(
        channel < temporal, 0, jnp.where(channel < temporal + spatial, temporal, temporal + spatial)
    )
    extent = jnp.where(channel < temporal, temporal, spatial)
    pair_index = (channel - part_start) // 2
    frequency = jnp.exp(
        -(2.0 * pair_index.astype(jnp.float32) / extent.astype(jnp.float32)) * math.log(rope_theta)
    )
    position = jnp.where(
        channel[None, :] < temporal,
        frames[:, None],
        jnp.where(channel[None, :] < temporal + spatial, grid_row[:, None], column[:, None]),
    )
    angles = position.astype(jnp.float32) * frequency[None, :]
    return (jnp.cos(angles), jnp.sin(angles))


def pack_kernel(blk_ref, v_ref, vdot_ref, out_ref, sems, *, xs, width):
    copies = []
    for i, x in enumerate(xs):
        columns = pl.ds(pl.multiple_of(blk_ref[x] * width, width), width)
        for a, ref in enumerate((v_ref, vdot_ref)):
            copies.append(
                pltpu.make_async_copy(
                    ref.at[0, :, columns], out_ref[i].at[a], sems.at[2 * i + a]
                )
            )
    for copy in copies:
        copy.start()
    for copy in copies:
        copy.wait()


def pack_values(blocks, value, vdot, xs, tokens, width):
    def kernel(blk_ref, v_ref, vdot_ref, *rest):
        pack_kernel(blk_ref, v_ref, vdot_ref, rest[:-1], rest[-1], xs=xs, width=width)

    return pl.pallas_call(
        kernel,
        out_shape=tuple(
            jax.ShapeDtypeStruct((2, tokens, width), jnp.bfloat16) for _ in xs
        ),
        in_specs=[
            pl.BlockSpec(memory_space=pltpu.SMEM),
            pl.BlockSpec(memory_space=pl.ANY),
            pl.BlockSpec(memory_space=pl.ANY),
        ],
        out_specs=tuple(pl.BlockSpec(memory_space=pltpu.VMEM) for _ in xs),
        scratch_shapes=[pltpu.SemaphoreType.DMA((2 * len(xs),))],
        cost_estimate=pl.CostEstimate(
            flops=0, bytes_accessed=8 * len(xs) * tokens * width, transcendentals=0
        ),
        name="pack_values",
    )(blocks, value, vdot)


def rope_kernel(blk_ref, q_ref, k_ref, qd_ref, kd_ref, cos_ref, sin_ref, *outs, n, chunks, heads):
    step = pl.program_id(0)
    cosine = cos_ref[...]
    sine = sin_ref[...]
    lane = lax.broadcasted_iota(jnp.int32, cosine.shape, 1)
    even = lane % 2 == 0
    sine_signed = jnp.where(even, -sine, sine)
    for x in range(n):

        @pl.when(step == x)
        def _(x=x):
            for a, ref in enumerate((q_ref, k_ref, qd_ref, kd_ref)):
                for c in range(chunks):
                    for j in range(heads):
                        at = (c * heads + j) * HD
                        t = ref[0, :, at : at + HD].astype(jnp.float32)
                        partner = jnp.where(
                            even, pltpu.roll(t, HD - 1, 1), pltpu.roll(t, 1, 1)
                        )
                        y = t * cosine + partner * sine_signed
                        outs[c * n + x][a, :, j * HD : (j + 1) * HD] = y.astype(jnp.bfloat16)


def rope_packs(blocks, q, k, qd, kd, cosine, sine, n, chunks, heads):
    tokens = q.shape[1]
    width = chunks * heads * HD
    column = pl.BlockSpec((1, tokens, width), lambda i, blk: (0, 0, blk[i]))
    table = pl.BlockSpec((tokens, HD), lambda i, blk: (0, 0))
    out = pl.BlockSpec((4, tokens, heads * HD), lambda i, blk: (0, 0, 0))
    return pl.pallas_call(
        functools.partial(rope_kernel, n=n, chunks=chunks, heads=heads),
        out_shape=tuple(
            jax.ShapeDtypeStruct((4, tokens, heads * HD), jnp.bfloat16) for _ in range(n * chunks)
        ),
        grid_spec=pltpu.PrefetchScalarGridSpec(
            num_scalar_prefetch=1,
            grid=(n,),
            in_specs=[column] * 4 + [table] * 2,
            out_specs=(out,) * (n * chunks),
        ),
        cost_estimate=pl.CostEstimate(
            flops=4 * tokens * n * width * 6,
            bytes_accessed=16 * tokens * n * width,
            transcendentals=0,
        ),
        name="rope_packs",
    )(blocks, q, k, qd, kd, cosine, sine)


def attend_kernel(blk_ref, v_ref, vd_ref, *refs, n):
    scaling = 1.0 / math.sqrt(HD)
    packs = refs[:n]
    values = refs[n : 2 * n - 1]
    outs = refs[2 * n - 1 :]
    nt = (((1,), (1,)), ((), ()))

    def dot(a, b):
        return jnp.dot(a, b, preferred_element_type=jnp.float32)

    def dot_t(a, b):
        return lax.dot_general(a, b, nt, preferred_element_type=jnp.float32)

    keys = jnp.concatenate([p[1] for p in packs], axis=0)
    kdots = jnp.concatenate([p[3] for p in packs], axis=0)
    both = jnp.concatenate([keys, kdots], axis=1)
    vals = jnp.concatenate([v_ref[0]] + [v[0] for v in values], axis=0)
    vdots = jnp.concatenate([vd_ref[0]] + [v[1] for v in values], axis=0)
    vboth = jnp.concatenate([vals, vdots], axis=1)
    for x in range(n):
        q = packs[x][0]
        qd = packs[x][2]
        raw = dot_t(q, keys)
        largest = jnp.max(raw, axis=-1, keepdims=True)
        expons = jnp.exp((raw - largest) * scaling)
        inverse = 1.0 / jnp.sum(expons, axis=-1, keepdims=True)
        weights = (expons * inverse).astype(jnp.bfloat16)
        scores_dot = dot_t(jnp.concatenate([qd, q], axis=1), both) * scaling
        product = weights.astype(jnp.float32) * scores_dot
        correction = jnp.sum(product, axis=-1, keepdims=True)
        mixed = dot(weights, vboth)
        out = mixed[:, :HD]
        tangent = mixed[:, HD:] + dot(product.astype(jnp.bfloat16), vals) - correction * out
        outs[x][0] = out.astype(jnp.bfloat16)
        outs[x][1] = tangent.astype(jnp.bfloat16)


def attend(blocks, value, vdot, packs, values, chunk, n, chunks, heads):
    tokens = value.shape[1]
    own = pl.BlockSpec(
        (1, tokens, HD), lambda j, blk: (0, 0, (blk[0] * chunks + chunk) * heads + j)
    )
    pack = pl.BlockSpec((4, tokens, HD), lambda j, blk: (0, 0, j))
    other = pl.BlockSpec((2, tokens, HD), lambda j, blk: (0, 0, chunk * heads + j))
    out = pl.BlockSpec((2, tokens, HD), lambda j, blk: (0, 0, j))
    pairs = (n * tokens) ** 2 * heads
    return pl.pallas_call(
        functools.partial(attend_kernel, n=n),
        out_shape=tuple(
            jax.ShapeDtypeStruct((2, tokens, heads * HD), jnp.bfloat16) for _ in range(n)
        ),
        grid_spec=pltpu.PrefetchScalarGridSpec(
            num_scalar_prefetch=1,
            grid=(heads,),
            in_specs=[own] * 2 + [pack] * n + [other] * (n - 1),
            out_specs=(out,) * n,
        ),
        cost_estimate=pl.CostEstimate(
            flops=12 * pairs * HD,
            bytes_accessed=16 * n * tokens * heads * HD,
            transcendentals=pairs,
        ),
        name="attend",
    )(blocks, value, vdot, *packs, *values)


def place_kernel(blk_ref, *refs, n, chunks, width):
    ins = refs[: n * chunks]
    outs = refs[n * chunks : n * chunks + 2]
    sems = refs[-1]
    copies = []
    for c in range(chunks):
        for x in range(n):
            first = pl.multiple_of((blk_ref[x] * chunks + c) * width, width)
            for a in range(2):
                copies.append(
                    pltpu.make_async_copy(
                        ins[c * n + x].at[a],
                        outs[a].at[0, :, pl.ds(first, width)],
                        sems.at[len(copies)],
                    )
                )
    for copy in copies:
        copy.start()
    for copy in copies:
        copy.wait()


def place(blocks, pieces, n, chunks, width, tokens):
    total = n * chunks * width
    shape = jax.ShapeDtypeStruct((1, tokens, total), jnp.bfloat16)
    return pl.pallas_call(
        functools.partial(place_kernel, n=n, chunks=chunks, width=width),
        out_shape=(shape, shape),
        in_specs=[pl.BlockSpec(memory_space=pltpu.SMEM)]
        + [pl.BlockSpec(memory_space=pltpu.VMEM)] * (n * chunks),
        out_specs=(pl.BlockSpec(memory_space=pl.ANY),) * 2,
        scratch_shapes=[pltpu.SemaphoreType.DMA((2 * n * chunks,))],
        cost_estimate=pl.CostEstimate(
            flops=0, bytes_accessed=8 * tokens * total, transcendentals=0
        ),
        name="place",
    )(blocks, *pieces)


def body_pairs(queries, key_states, value_states, query_tangent, key_tangent, value_tangent, offsets):
    n = lax.axis_size("seq")
    per_device = H // n
    chunks = 2 if per_device % 2 == 0 else 1
    heads = per_device // chunks
    tokens = queries.shape[1]
    width = per_device * HD
    me = lax.axis_index("seq")
    blocks = jnp.bitwise_xor(jnp.arange(n, dtype=jnp.int32), me.astype(jnp.int32))
    order = sorted(range(1, n), key=lambda x: (-(x.bit_length()), x))

    def swap(array, x):
        return lax.ppermute(array, "seq", [(i, i ^ x) for i in range(n)])

    value_in = {}
    for xs in (order[:1], order[1:]):
        if xs:
            sent = pack_values(blocks, value_states, value_tangent, xs, tokens, width)
            for x, array in zip(xs, sent):
                value_in[x] = swap(array, x)

    cosine, sine = rope_tables(offsets[0] + me * tokens, tokens)
    packs = rope_packs(
        blocks, queries, key_states, query_tangent, key_tangent, cosine, sine, n, chunks, heads
    )
    packs_in = []
    for c in range(chunks):
        mine = packs[c * n : (c + 1) * n]
        got = {x: swap(mine[x], x) for x in order}
        packs_in.append([mine[0]] + [got[x] for x in range(1, n)])
    pieces = []
    for c in range(chunks):
        outs = attend(
            blocks,
            value_states,
            value_tangent,
            packs_in[c],
            [value_in[x] for x in range(1, n)],
            c,
            n,
            chunks,
            heads,
        )
        got = {x: swap(outs[x], x) for x in order}
        pieces += [outs[0]] + [got[x] for x in range(1, n)]
    return place(blocks, pieces, n, chunks, heads * HD, tokens)


def rotate(tensor, cosine, sine):
    channel = jnp.arange(tensor.shape[-1], dtype=jnp.int32)
    partner = jnp.where(
        channel % 2 == 0, -jnp.roll(tensor, -1, axis=-1), jnp.roll(tensor, 1, axis=-1)
    )
    return (tensor * cosine + partner * sine).astype(jnp.bfloat16)


def primal_terms(query_blk, keys_all, values_all, scaling):
    scores = (
        jnp.einsum("bhd,khd->hbk", query_blk, keys_all, preferred_element_type=jnp.float32)
        * scaling
    )
    largest = jnp.max(scores, axis=-1, keepdims=True)
    expons = jnp.exp(scores - largest)
    probs = expons / jnp.sum(expons, axis=-1, keepdims=True)
    weights = probs.astype(jnp.bfloat16)
    out_full = jnp.einsum("hbk,khd->bhd", weights, values_all, preferred_element_type=jnp.float32)
    return (weights, out_full)


def tangent_terms(
    query_blk, qdot_blk, keys_all, kdots_all, values_all, vdots_all, weights, out_full, scaling
):
    scores_dot = (
        jnp.einsum("bhd,khd->hbk", qdot_blk, keys_all, preferred_element_type=jnp.float32)
        + jnp.einsum("bhd,khd->hbk", query_blk, kdots_all, preferred_element_type=jnp.float32)
    ) * scaling
    product = weights.astype(jnp.float32) * scores_dot
    correction = jnp.sum(product, axis=-1)
    product_half = product.astype(jnp.bfloat16)
    tangent = (
        jnp.einsum("hbk,khd->bhd", weights, vdots_all, preferred_element_type=jnp.float32)
        + jnp.einsum("hbk,khd->bhd", product_half, values_all, preferred_element_type=jnp.float32)
        - jnp.transpose(correction)[:, :, None] * out_full
    )
    return tangent.astype(jnp.bfloat16)


def body_general(queries, key_states, value_states, query_tangent, key_tangent, value_tangent, offsets):
    devices = lax.axis_size("seq")
    repeat = max(devices // H, 1)
    per_device = max(H // devices, 1)
    groups = H // per_device
    width = per_device * HD
    tokens = queries.shape[1]
    sub_rows = tokens // repeat
    scaling = 1.0 / math.sqrt(HD)
    first = offsets[0] + lax.axis_index("seq") * tokens
    cosine, sine = (t[:, None, :] for t in rope_tables(first, tokens))

    def roped(array):
        return rotate(array[0].reshape(tokens, H, HD).astype(jnp.float32), cosine, sine).reshape(
            tokens, H * HD
        )

    def by_rows(array):
        shaped = array.reshape(repeat, sub_rows, groups, width)
        return jnp.transpose(shaped, (2, 0, 1, 3)).reshape(devices, sub_rows, width)

    def by_copies(array):
        shaped = jnp.transpose(array.reshape(tokens, groups, width), (1, 0, 2))
        spread = jnp.broadcast_to(shaped[:, None], (groups, repeat, tokens, width))
        return spread.reshape(devices, tokens, width)

    query_send = by_rows(roped(queries))
    qdot_send = by_rows(roped(query_tangent))
    key_send = by_copies(roped(key_states))
    kdot_send = by_copies(roped(key_tangent))
    value_send = by_copies(value_states[0])
    vdot_send = by_copies(value_tangent[0])
    query_rows = devices * sub_rows
    block = min(512, query_rows)
    count = query_rows // block

    def heads_view(array):
        return array.reshape(array.shape[0], per_device, HD)

    def blocks(array):
        return array.reshape(count, block, per_device, HD)

    received = (
        lax.all_to_all(query_send, "seq", split_axis=0, concat_axis=1, tiled=True),
        lax.all_to_all(key_send, "seq", split_axis=0, concat_axis=1, tiled=True),
        lax.all_to_all(value_send, "seq", split_axis=0, concat_axis=1, tiled=True),
        lax.all_to_all(qdot_send, "seq", split_axis=0, concat_axis=1, tiled=True),
        lax.all_to_all(kdot_send, "seq", split_axis=0, concat_axis=1, tiled=True),
        lax.all_to_all(vdot_send, "seq", split_axis=0, concat_axis=1, tiled=True),
    )
    query_in, key_in, value_in, qdot_in, kdot_in, vdot_in = tuple((array[0] for array in received))
    keys_all, values_all = (heads_view(key_in), heads_view(value_in))
    kdots_all, vdots_all = (heads_view(kdot_in), heads_view(vdot_in))

    def one_block(parts):
        query_blk, qdot_blk = parts
        weights, out_full = primal_terms(query_blk, keys_all, values_all, scaling)
        tangent = tangent_terms(
            query_blk,
            qdot_blk,
            keys_all,
            kdots_all,
            values_all,
            vdots_all,
            weights,
            out_full,
            scaling,
        )
        return (out_full.astype(jnp.bfloat16), tangent)

    attended, tangent_out = lax.map(one_block, (blocks(query_in), blocks(qdot_in)))

    def to_sources(array):
        return array.reshape(devices, sub_rows, width)

    returned = (
        lax.all_to_all(to_sources(attended), "seq", split_axis=0, concat_axis=0, tiled=True),
        lax.all_to_all(to_sources(tangent_out), "seq", split_axis=0, concat_axis=0, tiled=True),
    )

    def to_tokens(array):
        shaped = array.reshape(groups, repeat, sub_rows, width)
        return jnp.transpose(shaped, (1, 2, 0, 3)).reshape(tokens, H * HD)[None]

    return (to_tokens(returned[0]), to_tokens(returned[1]))


def solution(mesh):
    in_specs = (
        P(("group", "clip"), "seq", None),
        P(("group", "clip"), "seq", None),
        P(("group", "clip"), "seq", None),
        P(("group", "clip"), "seq", None),
        P(("group", "clip"), "seq", None),
        P(("group", "clip"), "seq", None),
        P(("group", "clip")),
    )
    out_specs = (P(("group", "clip"), "seq", None), P(("group", "clip"), "seq", None))
    n = mesh.shape["seq"]
    whole_heads = n > 1 and n & (n - 1) == 0 and H % n == 0
    body = body_pairs if whole_heads else body_general
    return jax.shard_map(body, mesh=mesh, in_specs=in_specs, out_specs=out_specs, check_vma=False)
```

```python
import functools
import math

import jax
import jax.numpy as jnp
from jax import lax
from jax.experimental import pallas as pl
from jax.experimental.pallas import tpu as pltpu
from jax.sharding import PartitionSpec as P

H = 16
HD = 128
HH = 44
WW = 80


rope_theta = 10000.0


def rope_tables(first, count):
    global_index = first + jnp.arange(count, dtype=jnp.int32)
    frames = global_index // (HH * WW)
    grid_row = global_index // WW % HH
    column = global_index % WW
    spatial = HD // 6 * 2
    temporal = HD - 2 * spatial
    channel = jnp.arange(HD, dtype=jnp.int32)
    part_start = jnp.where(
        channel < temporal, 0, jnp.where(channel < temporal + spatial, temporal, temporal + spatial)
    )
    extent = jnp.where(channel < temporal, temporal, spatial)
    pair_index = (channel - part_start) // 2
    frequency = jnp.exp(
        -(2.0 * pair_index.astype(jnp.float32) / extent.astype(jnp.float32)) * math.log(rope_theta)
    )
    position = jnp.where(
        channel[None, :] < temporal,
        frames[:, None],
        jnp.where(channel[None, :] < temporal + spatial, grid_row[:, None], column[:, None]),
    )
    angles = position.astype(jnp.float32) * frequency[None, :]
    return (jnp.cos(angles), jnp.sin(angles))


def pack_values(value, vdot, wanted, tokens, width):
    count = sum(len(arrays) for _, arrays in wanted)

    def kernel(v_ref, vdot_ref, *rest):
        outs, sems = rest[:-1], rest[-1]
        me = lax.axis_index("seq")
        copies = []
        for out, (x, arrays) in zip(outs, wanted):
            columns = pl.ds(pl.multiple_of(jnp.bitwise_xor(me, x) * width, width), width)
            for i, a in enumerate(arrays):
                copies.append(
                    pltpu.make_async_copy(
                        (v_ref, vdot_ref)[a].at[0, :, columns], out.at[i], sems.at[len(copies)]
                    )
                )
        for copy in copies:
            copy.start()
        for copy in copies:
            copy.wait()

    return pl.pallas_call(
        kernel,
        out_shape=tuple(
            jax.ShapeDtypeStruct((len(arrays), tokens, width), jnp.bfloat16)
            for _, arrays in wanted
        ),
        in_specs=[pl.BlockSpec(memory_space=pltpu.HBM)] * 2,
        out_specs=tuple(pl.BlockSpec(memory_space=pltpu.VMEM) for _ in wanted),
        scratch_shapes=[pltpu.SemaphoreType.DMA((count,))],
        compiler_params=pltpu.CompilerParams(vmem_limit_bytes=8 << 20),
        cost_estimate=pl.CostEstimate(
            flops=0, bytes_accessed=4 * count * tokens * width, transcendentals=0
        ),
        name="pack_values",
    )(value, vdot)


def rope_kernel(blk_ref, q_ref, k_ref, qd_ref, kd_ref, cos_ref, sin_ref, *outs, n, chunks, heads):
    step = pl.program_id(0)
    cosine = cos_ref[...]
    sine = sin_ref[...]
    lane = lax.broadcasted_iota(jnp.int32, cosine.shape, 1)
    even = lane % 2 == 0
    sine_signed = jnp.where(even, -sine, sine)
    for x in range(n):

        @pl.when(step == x)
        def _(x=x):
            for a, ref in enumerate((q_ref, k_ref, qd_ref, kd_ref)):
                for c in range(chunks):
                    for j in range(heads):
                        at = (c * heads + j) * HD
                        t = ref[0, :, at : at + HD].astype(jnp.float32)
                        partner = jnp.where(
                            even, pltpu.roll(t, HD - 1, 1), pltpu.roll(t, 1, 1)
                        )
                        y = t * cosine + partner * sine_signed
                        outs[c * n + x][a, :, j * HD : (j + 1) * HD] = y.astype(jnp.bfloat16)


def rope_packs(blocks, q, k, qd, kd, cosine, sine, n, chunks, heads):
    tokens = q.shape[1]
    width = chunks * heads * HD
    column = pl.BlockSpec((1, tokens, width), lambda i, blk: (0, 0, blk[i]))
    table = pl.BlockSpec((tokens, HD), lambda i, blk: (0, 0))
    out = pl.BlockSpec((4, tokens, heads * HD), lambda i, blk: (0, 0, 0))
    return pl.pallas_call(
        functools.partial(rope_kernel, n=n, chunks=chunks, heads=heads),
        out_shape=tuple(
            jax.ShapeDtypeStruct((4, tokens, heads * HD), jnp.bfloat16) for _ in range(n * chunks)
        ),
        grid_spec=pltpu.PrefetchScalarGridSpec(
            num_scalar_prefetch=1,
            grid=(n,),
            in_specs=[column] * 4 + [table] * 2,
            out_specs=(out,) * (n * chunks),
        ),
        compiler_params=pltpu.CompilerParams(vmem_limit_bytes=24 << 20),
        cost_estimate=pl.CostEstimate(
            flops=4 * tokens * n * width * 6,
            bytes_accessed=16 * tokens * n * width,
            transcendentals=0,
        ),
        name="rope_packs",
    )(blocks, q, k, qd, kd, cosine, sine)


def attend_kernel(blk_ref, v_ref, vd_ref, *refs, n):
    scaling = 1.0 / math.sqrt(HD)
    packs = refs[:n]
    values = refs[n:-n]
    outs = refs[-n:]
    nt = (((1,), (1,)), ((), ()))

    def dot(a, b):
        return jnp.dot(a, b, preferred_element_type=jnp.float32)

    def dot_t(a, b):
        return lax.dot_general(a, b, nt, preferred_element_type=jnp.float32)

    keys = jnp.concatenate([p[1] for p in packs], axis=0)
    kdots = jnp.concatenate([p[3] for p in packs], axis=0)
    both = jnp.concatenate([keys, kdots], axis=1)
    rows = [v[i] for v in values for i in range(v.shape[0])]
    vals = jnp.concatenate([v_ref[0]] + rows[0::2], axis=0)
    vdots = jnp.concatenate([vd_ref[0]] + rows[1::2], axis=0)
    vboth = jnp.concatenate([vals, vdots], axis=1)
    for x in range(n):
        q = packs[x][0]
        qd = packs[x][2]
        raw = dot_t(q, keys)
        largest = jnp.max(raw, axis=-1, keepdims=True)
        expons = jnp.exp((raw - largest) * scaling)
        inverse = 1.0 / jnp.sum(expons, axis=-1, keepdims=True)
        weights = (expons * inverse).astype(jnp.bfloat16)
        scores_dot = dot_t(jnp.concatenate([qd, q], axis=1), both) * scaling
        product = weights.astype(jnp.float32) * scores_dot
        correction = jnp.sum(product, axis=-1, keepdims=True)
        mixed = dot(weights, vboth)
        out = mixed[:, :HD]
        tangent = mixed[:, HD:] + dot(product.astype(jnp.bfloat16), vals) - correction * out
        outs[x][0] = out.astype(jnp.bfloat16)
        outs[x][1] = tangent.astype(jnp.bfloat16)


def attend(blocks, value, vdot, packs, values, chunk, n, chunks, heads):
    tokens = value.shape[1]
    own = pl.BlockSpec(
        (1, tokens, HD), lambda j, blk: (0, 0, (blk[0] * chunks + chunk) * heads + j)
    )
    pack = pl.BlockSpec((4, tokens, HD), lambda j, blk: (0, 0, j))
    values = [array for arrays in values for array in arrays]
    others = [
        pl.BlockSpec((array.shape[0], tokens, HD), lambda j, blk: (0, 0, chunk * heads + j))
        for array in values
    ]
    out = pl.BlockSpec((2, tokens, HD), lambda j, blk: (0, 0, j))
    pairs = (n * tokens) ** 2 * heads
    return pl.pallas_call(
        functools.partial(attend_kernel, n=n),
        out_shape=tuple(
            jax.ShapeDtypeStruct((2, tokens, heads * HD), jnp.bfloat16) for _ in range(n)
        ),
        grid_spec=pltpu.PrefetchScalarGridSpec(
            num_scalar_prefetch=1,
            grid=(heads,),
            in_specs=[own] * 2 + [pack] * n + others,
            out_specs=(out,) * n,
        ),
        compiler_params=pltpu.CompilerParams(vmem_limit_bytes=24 << 20),
        cost_estimate=pl.CostEstimate(
            flops=12 * pairs * HD,
            bytes_accessed=16 * n * tokens * heads * HD,
            transcendentals=pairs,
        ),
        name="attend",
    )(blocks, value, vdot, *packs, *values)


def place(pieces, chunks, width, columns, tokens, into=None):
    shape = jax.ShapeDtypeStruct((1, tokens, columns), jnp.bfloat16)

    def kernel(*refs):
        ins, outs, sems = refs[: len(pieces)], refs[-3:-1], refs[-1]
        me = lax.axis_index("seq")
        copies = []
        for ref, (x, c, _) in zip(ins, pieces):
            first = (jnp.bitwise_xor(me, x) * chunks + c) * width
            for a in range(2):
                copies.append(
                    pltpu.make_async_copy(
                        ref.at[a],
                        outs[a].at[0, :, pl.ds(pl.multiple_of(first, width), width)],
                        sems.at[len(copies)],
                    )
                )
        for copy in copies:
            copy.start()
        for copy in copies:
            copy.wait()

    into = () if into is None else tuple(into)
    return pl.pallas_call(
        kernel,
        out_shape=(shape, shape),
        in_specs=[pl.BlockSpec(memory_space=pltpu.VMEM)] * len(pieces)
        + [pl.BlockSpec(memory_space=pl.ANY)] * len(into),
        out_specs=(pl.BlockSpec(memory_space=pl.ANY),) * 2,
        scratch_shapes=[pltpu.SemaphoreType.DMA((2 * len(pieces),))],
        input_output_aliases={len(pieces) + i: i for i in range(len(into))},
        compiler_params=pltpu.CompilerParams(vmem_limit_bytes=8 << 20),
        cost_estimate=pl.CostEstimate(
            flops=0, bytes_accessed=8 * len(pieces) * tokens * width, transcendentals=0
        ),
        name="place",
    )(*(piece for _, _, piece in pieces), *into)


def body_pairs(queries, key_states, value_states, query_tangent, key_tangent, value_tangent, offsets):
    n = lax.axis_size("seq")
    per_device = H // n
    chunks = 2 if per_device % 2 == 0 else 1
    heads = per_device // chunks
    tokens = queries.shape[1]
    width = per_device * HD
    me = lax.axis_index("seq")
    blocks = jnp.bitwise_xor(jnp.arange(n, dtype=jnp.int32), me.astype(jnp.int32))
    value_hbm = pltpu.with_memory_space_constraint(value_states, pltpu.HBM)
    vdot_hbm = pltpu.with_memory_space_constraint(value_tangent, pltpu.HBM)
    order = sorted(range(1, n), key=lambda x: (-(x.bit_length()), x))

    def swap(array, x):
        return lax.ppermute(array, "seq", [(i, i ^ x) for i in range(n)])

    value_in = {}
    for xs in (order[:1], order[1:]):
        wanted = [(x, (0, 1)) for x in xs]
        if wanted:
            for x, array in zip(xs, pack_values(value_hbm, vdot_hbm, wanted, tokens, width)):
                value_in[x] = (swap(array, x),)

    cosine, sine = rope_tables(offsets[0] + me * tokens, tokens)
    packs = rope_packs(
        blocks, queries, key_states, query_tangent, key_tangent, cosine, sine, n, chunks, heads
    )
    packs_in = []
    for c in range(chunks):
        mine = packs[c * n : (c + 1) * n]
        got = {x: swap(mine[x], x) for x in order}
        packs_in.append([mine[0]] + [got[x] for x in range(1, n)])
    early, late = [], []
    for c in range(chunks):
        outs = attend(
            blocks,
            value_states,
            value_tangent,
            packs_in[c],
            [value_in[x] for x in range(1, n)],
            c,
            n,
            chunks,
            heads,
        )
        early.append((0, c, outs[0]))
        last = early if c < chunks - 1 else late
        last += [(x, c, swap(outs[x], x)) for x in order]
    placed = place(early, chunks, heads * HD, H * HD, tokens)
    return place(late, chunks, heads * HD, H * HD, tokens, placed)


def rotate(tensor, cosine, sine):
    channel = jnp.arange(tensor.shape[-1], dtype=jnp.int32)
    partner = jnp.where(
        channel % 2 == 0, -jnp.roll(tensor, -1, axis=-1), jnp.roll(tensor, 1, axis=-1)
    )
    return (tensor * cosine + partner * sine).astype(jnp.bfloat16)


def primal_terms(query_blk, keys_all, values_all, scaling):
    scores = (
        jnp.einsum("bhd,khd->hbk", query_blk, keys_all, preferred_element_type=jnp.float32)
        * scaling
    )
    largest = jnp.max(scores, axis=-1, keepdims=True)
    expons = jnp.exp(scores - largest)
    probs = expons / jnp.sum(expons, axis=-1, keepdims=True)
    weights = probs.astype(jnp.bfloat16)
    out_full = jnp.einsum("hbk,khd->bhd", weights, values_all, preferred_element_type=jnp.float32)
    return (weights, out_full)


def tangent_terms(
    query_blk, qdot_blk, keys_all, kdots_all, values_all, vdots_all, weights, out_full, scaling
):
    scores_dot = (
        jnp.einsum("bhd,khd->hbk", qdot_blk, keys_all, preferred_element_type=jnp.float32)
        + jnp.einsum("bhd,khd->hbk", query_blk, kdots_all, preferred_element_type=jnp.float32)
    ) * scaling
    product = weights.astype(jnp.float32) * scores_dot
    correction = jnp.sum(product, axis=-1)
    product_half = product.astype(jnp.bfloat16)
    tangent = (
        jnp.einsum("hbk,khd->bhd", weights, vdots_all, preferred_element_type=jnp.float32)
        + jnp.einsum("hbk,khd->bhd", product_half, values_all, preferred_element_type=jnp.float32)
        - jnp.transpose(correction)[:, :, None] * out_full
    )
    return tangent.astype(jnp.bfloat16)


def body_general(queries, key_states, value_states, query_tangent, key_tangent, value_tangent, offsets):
    devices = lax.axis_size("seq")
    repeat = max(devices // H, 1)
    per_device = max(H // devices, 1)
    groups = H // per_device
    width = per_device * HD
    tokens = queries.shape[1]
    sub_rows = tokens // repeat
    scaling = 1.0 / math.sqrt(HD)
    first = offsets[0] + lax.axis_index("seq") * tokens
    cosine, sine = (t[:, None, :] for t in rope_tables(first, tokens))

    def roped(array):
        return rotate(array[0].reshape(tokens, H, HD).astype(jnp.float32), cosine, sine).reshape(
            tokens, H * HD
        )

    def by_rows(array):
        shaped = array.reshape(repeat, sub_rows, groups, width)
        return jnp.transpose(shaped, (2, 0, 1, 3)).reshape(devices, sub_rows, width)

    def by_copies(array):
        shaped = jnp.transpose(array.reshape(tokens, groups, width), (1, 0, 2))
        spread = jnp.broadcast_to(shaped[:, None], (groups, repeat, tokens, width))
        return spread.reshape(devices, tokens, width)

    query_send = by_rows(roped(queries))
    qdot_send = by_rows(roped(query_tangent))
    key_send = by_copies(roped(key_states))
    kdot_send = by_copies(roped(key_tangent))
    value_send = by_copies(value_states[0])
    vdot_send = by_copies(value_tangent[0])
    query_rows = devices * sub_rows
    block = min(512, query_rows)
    count = query_rows // block

    def heads_view(array):
        return array.reshape(array.shape[0], per_device, HD)

    def blocks(array):
        return array.reshape(count, block, per_device, HD)

    received = (
        lax.all_to_all(query_send, "seq", split_axis=0, concat_axis=1, tiled=True),
        lax.all_to_all(key_send, "seq", split_axis=0, concat_axis=1, tiled=True),
        lax.all_to_all(value_send, "seq", split_axis=0, concat_axis=1, tiled=True),
        lax.all_to_all(qdot_send, "seq", split_axis=0, concat_axis=1, tiled=True),
        lax.all_to_all(kdot_send, "seq", split_axis=0, concat_axis=1, tiled=True),
        lax.all_to_all(vdot_send, "seq", split_axis=0, concat_axis=1, tiled=True),
    )
    query_in, key_in, value_in, qdot_in, kdot_in, vdot_in = tuple((array[0] for array in received))
    keys_all, values_all = (heads_view(key_in), heads_view(value_in))
    kdots_all, vdots_all = (heads_view(kdot_in), heads_view(vdot_in))

    def one_block(parts):
        query_blk, qdot_blk = parts
        weights, out_full = primal_terms(query_blk, keys_all, values_all, scaling)
        tangent = tangent_terms(
            query_blk,
            qdot_blk,
            keys_all,
            kdots_all,
            values_all,
            vdots_all,
            weights,
            out_full,
            scaling,
        )
        return (out_full.astype(jnp.bfloat16), tangent)

    attended, tangent_out = lax.map(one_block, (blocks(query_in), blocks(qdot_in)))

    def to_sources(array):
        return array.reshape(devices, sub_rows, width)

    returned = (
        lax.all_to_all(to_sources(attended), "seq", split_axis=0, concat_axis=0, tiled=True),
        lax.all_to_all(to_sources(tangent_out), "seq", split_axis=0, concat_axis=0, tiled=True),
    )

    def to_tokens(array):
        shaped = array.reshape(groups, repeat, sub_rows, width)
        return jnp.transpose(shaped, (1, 2, 0, 3)).reshape(tokens, H * HD)[None]

    return (to_tokens(returned[0]), to_tokens(returned[1]))


def solution(mesh):
    in_specs = (
        P(("group", "clip"), "seq", None),
        P(("group", "clip"), "seq", None),
        P(("group", "clip"), "seq", None),
        P(("group", "clip"), "seq", None),
        P(("group", "clip"), "seq", None),
        P(("group", "clip"), "seq", None),
        P(("group", "clip")),
    )
    out_specs = (P(("group", "clip"), "seq", None), P(("group", "clip"), "seq", None))
    n = mesh.shape["seq"]
    whole_heads = n > 1 and n & (n - 1) == 0 and H % n == 0
    body = body_pairs if whole_heads else body_general
    return jax.shard_map(body, mesh=mesh, in_specs=in_specs, out_specs=out_specs, check_vma=False)
```

```python
import functools
import math

import jax
import jax.numpy as jnp
from jax import lax
from jax.experimental import pallas as pl
from jax.experimental.pallas import tpu as pltpu
from jax.sharding import PartitionSpec as P


H = 16
HD = 128
HH = 44
WW = 80


rope_theta = 10000.0

SIZES = (2, 2)
ORDERS = {'v': (2, 3, 1), 'qk': (1, 2, 3), 'out': (3, 2, 1)}


def rope_tables(first, count):
    global_index = first + jnp.arange(count, dtype=jnp.int32)
    frames = global_index // (HH * WW)
    grid_row = global_index // WW % HH
    column = global_index % WW
    spatial = HD // 6 * 2
    temporal = HD - 2 * spatial
    channel = jnp.arange(HD, dtype=jnp.int32)
    part_start = jnp.where(
        channel < temporal, 0, jnp.where(channel < temporal + spatial, temporal, temporal + spatial)
    )
    extent = jnp.where(channel < temporal, temporal, spatial)
    pair_index = (channel - part_start) // 2
    frequency = jnp.exp(
        -(2.0 * pair_index.astype(jnp.float32) / extent.astype(jnp.float32)) * math.log(rope_theta)
    )
    position = jnp.where(
        channel[None, :] < temporal,
        frames[:, None],
        jnp.where(channel[None, :] < temporal + spatial, grid_row[:, None], column[:, None]),
    )
    angles = position.astype(jnp.float32) * frequency[None, :]
    return (jnp.cos(angles), jnp.sin(angles))


def pack_values(value, vdot, wanted, tokens, width):
    count = sum(len(arrays) for _, arrays in wanted)

    def kernel(v_ref, vdot_ref, *rest):
        outs, sems = rest[:-1], rest[-1]
        me = lax.axis_index("seq")
        copies = []
        for out, (x, arrays) in zip(outs, wanted):
            columns = pl.ds(pl.multiple_of(jnp.bitwise_xor(me, x) * width, width), width)
            for i, a in enumerate(arrays):
                copies.append(
                    pltpu.make_async_copy(
                        (v_ref, vdot_ref)[a].at[0, :, columns], out.at[i], sems.at[len(copies)]
                    )
                )
        for copy in copies:
            copy.start()
        for copy in copies:
            copy.wait()

    return pl.pallas_call(
        kernel,
        out_shape=tuple(
            jax.ShapeDtypeStruct((len(arrays), tokens, width), jnp.bfloat16)
            for _, arrays in wanted
        ),
        in_specs=[pl.BlockSpec(memory_space=pltpu.HBM)] * 2,
        out_specs=tuple(pl.BlockSpec(memory_space=pltpu.VMEM) for _ in wanted),
        scratch_shapes=[pltpu.SemaphoreType.DMA((count,))],
        compiler_params=pltpu.CompilerParams(vmem_limit_bytes=8 << 20),
        cost_estimate=pl.CostEstimate(
            flops=0, bytes_accessed=4 * count * tokens * width, transcendentals=0
        ),
        name="pack_values",
    )(value, vdot)


def rope_kernel(blk_ref, q_ref, k_ref, qd_ref, kd_ref, cos_ref, sin_ref, *outs, n, sizes):
    step = pl.program_id(0)
    cosine = cos_ref[...]
    sine = sin_ref[...]
    lane = lax.broadcasted_iota(jnp.int32, cosine.shape, 1)
    even = lane % 2 == 0
    sine_signed = jnp.where(even, -sine, sine)
    for x in range(n):

        @pl.when(step == x)
        def _(x=x):
            for a, ref in enumerate((q_ref, k_ref, qd_ref, kd_ref)):
                for c, heads in enumerate(sizes):
                    for j in range(heads):
                        at = (sum(sizes[:c]) + j) * HD
                        t = ref[0, :, at : at + HD].astype(jnp.float32)
                        partner = jnp.where(
                            even, pltpu.roll(t, HD - 1, 1), pltpu.roll(t, 1, 1)
                        )
                        y = t * cosine + partner * sine_signed
                        outs[c * n + x][a, :, j * HD : (j + 1) * HD] = y.astype(jnp.bfloat16)


def rope_packs(blocks, q, k, qd, kd, cosine, sine, n, sizes):
    tokens = q.shape[1]
    width = sum(sizes) * HD
    column = pl.BlockSpec((1, tokens, width), lambda i, blk: (0, 0, blk[i]))
    table = pl.BlockSpec((tokens, HD), lambda i, blk: (0, 0))
    shapes = [(4, tokens, heads * HD) for heads in sizes for _ in range(n)]
    return pl.pallas_call(
        functools.partial(rope_kernel, n=n, sizes=sizes),
        out_shape=tuple(jax.ShapeDtypeStruct(shape, jnp.bfloat16) for shape in shapes),
        grid_spec=pltpu.PrefetchScalarGridSpec(
            num_scalar_prefetch=1,
            grid=(n,),
            in_specs=[column] * 4 + [table] * 2,
            out_specs=tuple(pl.BlockSpec(shape, lambda i, blk: (0, 0, 0)) for shape in shapes),
        ),
        compiler_params=pltpu.CompilerParams(vmem_limit_bytes=24 << 20),
        cost_estimate=pl.CostEstimate(
            flops=4 * tokens * n * width * 6,
            bytes_accessed=16 * tokens * n * width,
            transcendentals=0,
        ),
        name="rope_packs",
    )(blocks, q, k, qd, kd, cosine, sine)


def attend_kernel(blk_ref, v_ref, vd_ref, *refs, n):
    scaling = 1.0 / math.sqrt(HD)
    packs = refs[:n]
    values = refs[n:-n]
    outs = refs[-n:]
    nt = (((1,), (1,)), ((), ()))

    def dot(a, b):
        return jnp.dot(a, b, preferred_element_type=jnp.float32)

    def dot_t(a, b):
        return lax.dot_general(a, b, nt, preferred_element_type=jnp.float32)

    keys = jnp.concatenate([p[1] for p in packs], axis=0)
    kdots = jnp.concatenate([p[3] for p in packs], axis=0)
    both = jnp.concatenate([keys, kdots], axis=1)
    rows = [v[i] for v in values for i in range(v.shape[0])]
    vals = jnp.concatenate([v_ref[0]] + rows[0::2], axis=0)
    vdots = jnp.concatenate([vd_ref[0]] + rows[1::2], axis=0)
    vboth = jnp.concatenate([vals, vdots], axis=1)
    for x in range(n):
        q = packs[x][0]
        qd = packs[x][2]
        raw = dot_t(q, keys)
        largest = jnp.max(raw, axis=-1, keepdims=True)
        expons = jnp.exp((raw - largest) * scaling)
        inverse = 1.0 / jnp.sum(expons, axis=-1, keepdims=True)
        weights = (expons * inverse).astype(jnp.bfloat16)
        scores_dot = dot_t(jnp.concatenate([qd, q], axis=1), both) * scaling
        product = weights.astype(jnp.float32) * scores_dot
        correction = jnp.sum(product, axis=-1, keepdims=True)
        mixed = dot(weights, vboth)
        out = mixed[:, :HD]
        tangent = mixed[:, HD:] + dot(product.astype(jnp.bfloat16), vals) - correction * out
        outs[x][0] = out.astype(jnp.bfloat16)
        outs[x][1] = tangent.astype(jnp.bfloat16)


def attend(blocks, value, vdot, packs, values, start, heads, n):
    tokens = value.shape[1]
    per_device = H // n
    own = pl.BlockSpec(
        (1, tokens, HD), lambda j, blk: (0, 0, blk[0] * per_device + start + j)
    )
    pack = pl.BlockSpec((4, tokens, HD), lambda j, blk: (0, 0, j))
    values = [array for arrays in values for array in arrays]
    others = [
        pl.BlockSpec((array.shape[0], tokens, HD), lambda j, blk: (0, 0, start + j))
        for array in values
    ]
    out = pl.BlockSpec((2, tokens, HD), lambda j, blk: (0, 0, j))
    pairs = (n * tokens) ** 2 * heads
    return pl.pallas_call(
        functools.partial(attend_kernel, n=n),
        out_shape=tuple(
            jax.ShapeDtypeStruct((2, tokens, heads * HD), jnp.bfloat16) for _ in range(n)
        ),
        grid_spec=pltpu.PrefetchScalarGridSpec(
            num_scalar_prefetch=1,
            grid=(heads,),
            in_specs=[own] * 2 + [pack] * n + others,
            out_specs=(out,) * n,
        ),
        compiler_params=pltpu.CompilerParams(vmem_limit_bytes=24 << 20),
        cost_estimate=pl.CostEstimate(
            flops=12 * pairs * HD,
            bytes_accessed=16 * n * tokens * heads * HD,
            transcendentals=pairs,
        ),
        name="attend",
    )(blocks, value, vdot, *packs, *values)


def place(pieces, width, tokens, into=None):
    shape = jax.ShapeDtypeStruct((1, tokens, H * HD), jnp.bfloat16)
    total = sum(piece.shape[2] for _, _, piece in pieces)

    def kernel(*refs):
        ins, outs, sems = refs[: len(pieces)], refs[-3:-1], refs[-1]
        me = lax.axis_index("seq")
        copies = []
        for ref, (x, column, _) in zip(ins, pieces):
            first = pl.multiple_of(jnp.bitwise_xor(me, x) * width + column, HD)
            for a in range(2):
                copies.append(
                    pltpu.make_async_copy(
                        ref.at[a],
                        outs[a].at[0, :, pl.ds(first, ref.shape[2])],
                        sems.at[len(copies)],
                    )
                )
        for copy in copies:
            copy.start()
        for copy in copies:
            copy.wait()

    into = () if into is None else tuple(into)
    return pl.pallas_call(
        kernel,
        out_shape=(shape, shape),
        in_specs=[pl.BlockSpec(memory_space=pltpu.VMEM)] * len(pieces)
        + [pl.BlockSpec(memory_space=pl.ANY)] * len(into),
        out_specs=(pl.BlockSpec(memory_space=pl.ANY),) * 2,
        scratch_shapes=[pltpu.SemaphoreType.DMA((2 * len(pieces),))],
        input_output_aliases={len(pieces) + i: i for i in range(len(into))},
        compiler_params=pltpu.CompilerParams(vmem_limit_bytes=8 << 20),
        cost_estimate=pl.CostEstimate(
            flops=0, bytes_accessed=8 * tokens * total, transcendentals=0
        ),
        name="place",
    )(*(piece for _, _, piece in pieces), *into)


def chunk_sizes(n):
    per_device = H // n
    return SIZES if per_device == 4 else (1,) * per_device


def partner_order(n, kind):
    middle_first = sorted(range(1, n), key=lambda x: (-x.bit_length(), x))
    return [x for x in ORDERS[kind] if x < n] if n == 4 else middle_first


def body_pairs(*args):
    return pairs_program(*args)


def pairs_program(queries, key_states, value_states, query_tangent, key_tangent, value_tangent, offsets):
    n = lax.axis_size("seq")
    order = partner_order(n, "v")
    sizes = chunk_sizes(n)
    starts = [sum(sizes[:c]) for c in range(len(sizes))]
    tokens = queries.shape[1]
    width = H // n * HD
    me = lax.axis_index("seq")
    value_hbm = pltpu.with_memory_space_constraint(value_states, pltpu.HBM)
    vdot_hbm = pltpu.with_memory_space_constraint(value_tangent, pltpu.HBM)

    def swap(array, x):
        return lax.ppermute(array, "seq", [(i, i ^ x) for i in range(n)])

    value_in = {}
    for xs in (order[:1], order[1:]):
        wanted = [(x, (0, 1)) for x in xs]
        if wanted:
            sent = pack_values(value_hbm, vdot_hbm, wanted, tokens, width)
            for x, array in zip(xs, sent):
                value_in[x] = (swap(array, x),)

    blocks = jnp.bitwise_xor(jnp.arange(n, dtype=jnp.int32), me.astype(jnp.int32))
    cosine, sine = rope_tables(offsets[0] + me * tokens, tokens)
    packs = rope_packs(
        blocks, queries, key_states, query_tangent, key_tangent, cosine, sine, n, sizes
    )
    packs_in = []
    for c in range(len(sizes)):
        mine = packs[c * n : (c + 1) * n]
        got = {x: swap(mine[x], x) for x in partner_order(n, "qk")}
        packs_in.append([mine[0]] + [got[x] for x in range(1, n)])
    early, late = [], []
    for c, (start, heads) in enumerate(zip(starts, sizes)):
        outs = attend(
            blocks,
            value_states,
            value_tangent,
            packs_in[c],
            [value_in[x] for x in range(1, n)],
            start,
            heads,
            n,
        )
        early.append((0, start * HD, outs[0]))
        last = early if c < len(sizes) - 1 else late
        last += [(x, start * HD, swap(outs[x], x)) for x in partner_order(n, "out")]
    placed = place(early, width, tokens)
    return place(late, width, tokens, placed)


def rotate(tensor, cosine, sine):
    channel = jnp.arange(tensor.shape[-1], dtype=jnp.int32)
    partner = jnp.where(
        channel % 2 == 0, -jnp.roll(tensor, -1, axis=-1), jnp.roll(tensor, 1, axis=-1)
    )
    return (tensor * cosine + partner * sine).astype(jnp.bfloat16)


def primal_terms(query_blk, keys_all, values_all, scaling):
    scores = (
        jnp.einsum("bhd,khd->hbk", query_blk, keys_all, preferred_element_type=jnp.float32)
        * scaling
    )
    largest = jnp.max(scores, axis=-1, keepdims=True)
    expons = jnp.exp(scores - largest)
    probs = expons / jnp.sum(expons, axis=-1, keepdims=True)
    weights = probs.astype(jnp.bfloat16)
    out_full = jnp.einsum("hbk,khd->bhd", weights, values_all, preferred_element_type=jnp.float32)
    return (weights, out_full)


def tangent_terms(
    query_blk, qdot_blk, keys_all, kdots_all, values_all, vdots_all, weights, out_full, scaling
):
    scores_dot = (
        jnp.einsum("bhd,khd->hbk", qdot_blk, keys_all, preferred_element_type=jnp.float32)
        + jnp.einsum("bhd,khd->hbk", query_blk, kdots_all, preferred_element_type=jnp.float32)
    ) * scaling
    product = weights.astype(jnp.float32) * scores_dot
    correction = jnp.sum(product, axis=-1)
    product_half = product.astype(jnp.bfloat16)
    tangent = (
        jnp.einsum("hbk,khd->bhd", weights, vdots_all, preferred_element_type=jnp.float32)
        + jnp.einsum("hbk,khd->bhd", product_half, values_all, preferred_element_type=jnp.float32)
        - jnp.transpose(correction)[:, :, None] * out_full
    )
    return tangent.astype(jnp.bfloat16)


def body_general(queries, key_states, value_states, query_tangent, key_tangent, value_tangent, offsets):
    devices = lax.axis_size("seq")
    repeat = max(devices // H, 1)
    per_device = max(H // devices, 1)
    groups = H // per_device
    width = per_device * HD
    tokens = queries.shape[1]
    sub_rows = tokens // repeat
    scaling = 1.0 / math.sqrt(HD)
    first = offsets[0] + lax.axis_index("seq") * tokens
    cosine, sine = (t[:, None, :] for t in rope_tables(first, tokens))

    def roped(array):
        return rotate(array[0].reshape(tokens, H, HD).astype(jnp.float32), cosine, sine).reshape(
            tokens, H * HD
        )

    def by_rows(array):
        shaped = array.reshape(repeat, sub_rows, groups, width)
        return jnp.transpose(shaped, (2, 0, 1, 3)).reshape(devices, sub_rows, width)

    def by_copies(array):
        shaped = jnp.transpose(array.reshape(tokens, groups, width), (1, 0, 2))
        spread = jnp.broadcast_to(shaped[:, None], (groups, repeat, tokens, width))
        return spread.reshape(devices, tokens, width)

    query_send = by_rows(roped(queries))
    qdot_send = by_rows(roped(query_tangent))
    key_send = by_copies(roped(key_states))
    kdot_send = by_copies(roped(key_tangent))
    value_send = by_copies(value_states[0])
    vdot_send = by_copies(value_tangent[0])
    query_rows = devices * sub_rows
    block = min(512, query_rows)
    count = query_rows // block

    def heads_view(array):
        return array.reshape(array.shape[0], per_device, HD)

    def blocks(array):
        return array.reshape(count, block, per_device, HD)

    received = (
        lax.all_to_all(query_send, "seq", split_axis=0, concat_axis=1, tiled=True),
        lax.all_to_all(key_send, "seq", split_axis=0, concat_axis=1, tiled=True),
        lax.all_to_all(value_send, "seq", split_axis=0, concat_axis=1, tiled=True),
        lax.all_to_all(qdot_send, "seq", split_axis=0, concat_axis=1, tiled=True),
        lax.all_to_all(kdot_send, "seq", split_axis=0, concat_axis=1, tiled=True),
        lax.all_to_all(vdot_send, "seq", split_axis=0, concat_axis=1, tiled=True),
    )
    query_in, key_in, value_in, qdot_in, kdot_in, vdot_in = tuple((array[0] for array in received))
    keys_all, values_all = (heads_view(key_in), heads_view(value_in))
    kdots_all, vdots_all = (heads_view(kdot_in), heads_view(vdot_in))

    def one_block(parts):
        query_blk, qdot_blk = parts
        weights, out_full = primal_terms(query_blk, keys_all, values_all, scaling)
        tangent = tangent_terms(
            query_blk,
            qdot_blk,
            keys_all,
            kdots_all,
            values_all,
            vdots_all,
            weights,
            out_full,
            scaling,
        )
        return (out_full.astype(jnp.bfloat16), tangent)

    attended, tangent_out = lax.map(one_block, (blocks(query_in), blocks(qdot_in)))

    def to_sources(array):
        return array.reshape(devices, sub_rows, width)

    returned = (
        lax.all_to_all(to_sources(attended), "seq", split_axis=0, concat_axis=0, tiled=True),
        lax.all_to_all(to_sources(tangent_out), "seq", split_axis=0, concat_axis=0, tiled=True),
    )

    def to_tokens(array):
        shaped = array.reshape(groups, repeat, sub_rows, width)
        return jnp.transpose(shaped, (1, 2, 0, 3)).reshape(tokens, H * HD)[None]

    return (to_tokens(returned[0]), to_tokens(returned[1]))


def solution(mesh):
    in_specs = (
        P(("group", "clip"), "seq", None),
        P(("group", "clip"), "seq", None),
        P(("group", "clip"), "seq", None),
        P(("group", "clip"), "seq", None),
        P(("group", "clip"), "seq", None),
        P(("group", "clip"), "seq", None),
        P(("group", "clip")),
    )
    out_specs = (P(("group", "clip"), "seq", None), P(("group", "clip"), "seq", None))
    n = mesh.shape["seq"]
    whole_heads = n > 1 and n & (n - 1) == 0 and H % n == 0
    body = body_pairs if whole_heads else body_general
    return jax.shard_map(body, mesh=mesh, in_specs=in_specs, out_specs=out_specs, check_vma=False)
```

```python
import functools
import math

import jax
import jax.numpy as jnp
from jax import lax
from jax.experimental import pallas as pl
from jax.experimental.pallas import tpu as pltpu
from jax.sharding import PartitionSpec as P


H = 16
HD = 128
HH = 44
WW = 80


rope_theta = 10000.0

SIZES = (2, 2)
ORDERS = {"v": (3, 2, 1), "qk": (2, 3, 1), "out": (3, 2, 1)}
LAST = ((3, (0, 3)), (2, None), (1, None), (3, (1, 2)))


def rope_tables(first, count):
    global_index = first + jnp.arange(count, dtype=jnp.int32)
    frames = global_index // (HH * WW)
    grid_row = global_index // WW % HH
    column = global_index % WW
    spatial = HD // 6 * 2
    temporal = HD - 2 * spatial
    channel = jnp.arange(HD, dtype=jnp.int32)
    part_start = jnp.where(
        channel < temporal, 0, jnp.where(channel < temporal + spatial, temporal, temporal + spatial)
    )
    extent = jnp.where(channel < temporal, temporal, spatial)
    pair_index = (channel - part_start) // 2
    frequency = jnp.exp(
        -(2.0 * pair_index.astype(jnp.float32) / extent.astype(jnp.float32)) * math.log(rope_theta)
    )
    position = jnp.where(
        channel[None, :] < temporal,
        frames[:, None],
        jnp.where(channel[None, :] < temporal + spatial, grid_row[:, None], column[:, None]),
    )
    angles = position.astype(jnp.float32) * frequency[None, :]
    return (jnp.cos(angles), jnp.sin(angles))


def pack_values(value, vdot, wanted, tokens, width):
    count = sum(len(arrays) for _, arrays in wanted)

    def kernel(v_ref, vdot_ref, *rest):
        outs, sems = rest[:-1], rest[-1]
        me = lax.axis_index("seq")
        copies = []
        for out, (x, arrays) in zip(outs, wanted):
            columns = pl.ds(pl.multiple_of(jnp.bitwise_xor(me, x) * width, width), width)
            for i, a in enumerate(arrays):
                copies.append(
                    pltpu.make_async_copy(
                        (v_ref, vdot_ref)[a].at[0, :, columns], out.at[i], sems.at[len(copies)]
                    )
                )
        for copy in copies:
            copy.start()
        for copy in copies:
            copy.wait()

    return pl.pallas_call(
        kernel,
        out_shape=tuple(
            jax.ShapeDtypeStruct((len(arrays), tokens, width), jnp.bfloat16)
            for _, arrays in wanted
        ),
        in_specs=[pl.BlockSpec(memory_space=pltpu.HBM)] * 2,
        out_specs=tuple(pl.BlockSpec(memory_space=pltpu.VMEM) for _ in wanted),
        scratch_shapes=[pltpu.SemaphoreType.DMA((count,))],
        compiler_params=pltpu.CompilerParams(vmem_limit_bytes=8 << 20),
        cost_estimate=pl.CostEstimate(
            flops=0, bytes_accessed=4 * count * tokens * width, transcendentals=0
        ),
        name="pack_values",
    )(value, vdot)


def rope_kernel(blk_ref, q_ref, k_ref, qd_ref, kd_ref, cos_ref, sin_ref, *outs, n, sizes):
    step = pl.program_id(0)
    cosine = cos_ref[...]
    sine = sin_ref[...]
    lane = lax.broadcasted_iota(jnp.int32, cosine.shape, 1)
    even = lane % 2 == 0
    sine_signed = jnp.where(even, -sine, sine)
    for x in range(n):

        @pl.when(step == x)
        def _(x=x):
            for a, ref in enumerate((q_ref, k_ref, qd_ref, kd_ref)):
                for c, heads in enumerate(sizes):
                    for j in range(heads):
                        at = (sum(sizes[:c]) + j) * HD
                        t = ref[0, :, at : at + HD].astype(jnp.float32)
                        partner = jnp.where(
                            even, pltpu.roll(t, HD - 1, 1), pltpu.roll(t, 1, 1)
                        )
                        y = t * cosine + partner * sine_signed
                        outs[c * n + x][a, :, j * HD : (j + 1) * HD] = y.astype(jnp.bfloat16)


def rope_packs(blocks, q, k, qd, kd, cosine, sine, n, sizes):
    tokens = q.shape[1]
    width = sum(sizes) * HD
    column = pl.BlockSpec((1, tokens, width), lambda i, blk: (0, 0, blk[i]))
    table = pl.BlockSpec((tokens, HD), lambda i, blk: (0, 0))
    shapes = [(4, tokens, heads * HD) for heads in sizes for _ in range(n)]
    return pl.pallas_call(
        functools.partial(rope_kernel, n=n, sizes=sizes),
        out_shape=tuple(jax.ShapeDtypeStruct(shape, jnp.bfloat16) for shape in shapes),
        grid_spec=pltpu.PrefetchScalarGridSpec(
            num_scalar_prefetch=1,
            grid=(n,),
            in_specs=[column] * 4 + [table] * 2,
            out_specs=tuple(pl.BlockSpec(shape, lambda i, blk: (0, 0, 0)) for shape in shapes),
        ),
        compiler_params=pltpu.CompilerParams(vmem_limit_bytes=24 << 20),
        cost_estimate=pl.CostEstimate(
            flops=4 * tokens * n * width * 6,
            bytes_accessed=16 * tokens * n * width,
            transcendentals=0,
        ),
        name="rope_packs",
    )(blocks, q, k, qd, kd, cosine, sine)


def attend_kernel(blk_ref, v_ref, vd_ref, *refs, n):
    scaling = 1.0 / math.sqrt(HD)
    packs = refs[:n]
    values = refs[n:-n]
    outs = refs[-n:]
    nt = (((1,), (1,)), ((), ()))

    def dot(a, b):
        return jnp.dot(a, b, preferred_element_type=jnp.float32)

    def dot_t(a, b):
        return lax.dot_general(a, b, nt, preferred_element_type=jnp.float32)

    keys = jnp.concatenate([p[1] for p in packs], axis=0)
    kdots = jnp.concatenate([p[3] for p in packs], axis=0)
    both = jnp.concatenate([keys, kdots], axis=1)
    rows = [v[i] for v in values for i in range(v.shape[0])]
    vals = jnp.concatenate([v_ref[0]] + rows[0::2], axis=0)
    vdots = jnp.concatenate([vd_ref[0]] + rows[1::2], axis=0)
    vboth = jnp.concatenate([vals, vdots], axis=1)
    q = jnp.concatenate([p[0] for p in packs], axis=0)
    qd = jnp.concatenate([p[2] for p in packs], axis=0)
    raw = dot_t(q, keys)
    largest = jnp.max(raw, axis=-1, keepdims=True)
    expons = jnp.exp2((raw - largest) * (scaling * math.log2(math.e)))
    inverse = 1.0 / jnp.sum(expons, axis=-1, keepdims=True)
    weights = (expons * inverse).astype(jnp.bfloat16)
    scores_dot = dot_t(jnp.concatenate([qd, q], axis=1), both) * scaling
    product = weights.astype(jnp.float32) * scores_dot
    correction = jnp.sum(product, axis=-1, keepdims=True)
    mixed = dot(weights, vboth)
    out = mixed[:, :HD]
    tangent = mixed[:, HD:] + dot(product.astype(jnp.bfloat16), vals) - correction * out
    rows = out.shape[0] // n
    for x in range(n):
        outs[x][0] = out[x * rows : (x + 1) * rows].astype(jnp.bfloat16)
        outs[x][1] = tangent[x * rows : (x + 1) * rows].astype(jnp.bfloat16)


def attend(blocks, value, vdot, packs, values, start, heads, n):
    tokens = value.shape[1]
    per_device = H // n
    own = pl.BlockSpec(
        (1, tokens, HD), lambda j, blk: (0, 0, blk[0] * per_device + start + j)
    )
    pack = pl.BlockSpec((4, tokens, HD), lambda j, blk: (0, 0, j))
    values = [array for arrays in values for array in arrays]
    others = [
        pl.BlockSpec((array.shape[0], tokens, HD), lambda j, blk: (0, 0, start + j))
        for array in values
    ]
    out = pl.BlockSpec((2, tokens, HD), lambda j, blk: (0, 0, j))
    pairs = (n * tokens) ** 2 * heads
    return pl.pallas_call(
        functools.partial(attend_kernel, n=n),
        out_shape=tuple(
            jax.ShapeDtypeStruct((2, tokens, heads * HD), jnp.bfloat16) for _ in range(n)
        ),
        grid_spec=pltpu.PrefetchScalarGridSpec(
            num_scalar_prefetch=1,
            grid=(heads,),
            in_specs=[own] * 2 + [pack] * n + others,
            out_specs=(out,) * n,
        ),
        compiler_params=pltpu.CompilerParams(vmem_limit_bytes=24 << 20),
        cost_estimate=pl.CostEstimate(
            flops=12 * pairs * HD,
            bytes_accessed=16 * n * tokens * heads * HD,
            transcendentals=pairs,
        ),
        name="attend",
    )(blocks, value, vdot, *packs, *values)


def place(pieces, width, tokens, into=None):
    shape = jax.ShapeDtypeStruct((1, tokens, H * HD), jnp.bfloat16)
    total = sum(piece[2].shape[2] for piece in pieces)

    def kernel(*refs):
        ins, outs, sems = refs[: len(pieces)], refs[-3:-1], refs[-1]
        me = lax.axis_index("seq")
        for act in ("start", "wait"):
            for i, (ref, (x, column, _, members)) in enumerate(zip(ins, pieces)):

                def copies(i=i, ref=ref, x=x, column=column):
                    first = pl.multiple_of(jnp.bitwise_xor(me, x) * width + column, HD)
                    for a in range(2):
                        copy = pltpu.make_async_copy(
                            ref.at[a],
                            outs[a].at[0, :, pl.ds(first, ref.shape[2])],
                            sems.at[2 * i + a],
                        )
                        getattr(copy, act)()

                if members is None:
                    copies()
                else:
                    pl.when(functools.reduce(jnp.logical_or, [me == m for m in members]))(copies)

    into = () if into is None else tuple(into)
    return pl.pallas_call(
        kernel,
        out_shape=(shape, shape),
        in_specs=[pl.BlockSpec(memory_space=pltpu.VMEM)] * len(pieces)
        + [pl.BlockSpec(memory_space=pl.ANY)] * len(into),
        out_specs=(pl.BlockSpec(memory_space=pl.ANY),) * 2,
        scratch_shapes=[pltpu.SemaphoreType.DMA((2 * len(pieces),))],
        input_output_aliases={len(pieces) + i: i for i in range(len(into))},
        compiler_params=pltpu.CompilerParams(vmem_limit_bytes=8 << 20),
        cost_estimate=pl.CostEstimate(
            flops=0, bytes_accessed=8 * tokens * total, transcendentals=0
        ),
        name="place",
    )(*(piece[2] for piece in pieces), *into)


def chunk_sizes(n):
    per_device = H // n
    return SIZES if per_device == 4 else (1,) * per_device


def routes(n, chunk):
    if n == 4 and chunk == len(chunk_sizes(n)) - 1:
        return LAST
    return [(x, None) for x in partner_order(n, "out")]


def partner_order(n, kind):
    middle_first = sorted(range(1, n), key=lambda x: (-x.bit_length(), x))
    return [x for x in ORDERS[kind] if x < n] if n == 4 else middle_first


def body_pairs(*args):
    return pairs_program(*args)


def pairs_program(queries, key_states, value_states, query_tangent, key_tangent, value_tangent, offsets):
    n = lax.axis_size("seq")
    order = partner_order(n, "v")
    sizes = chunk_sizes(n)
    starts = [sum(sizes[:c]) for c in range(len(sizes))]
    tokens = queries.shape[1]
    width = H // n * HD
    me = lax.axis_index("seq")
    value_hbm = pltpu.with_memory_space_constraint(value_states, pltpu.HBM)
    vdot_hbm = pltpu.with_memory_space_constraint(value_tangent, pltpu.HBM)

    def swap(array, x, members=None):
        pairs = [(i ^ x, i) for i in range(n) if members is None or i in members]
        return lax.ppermute(array, "seq", pairs)

    first, rest = order[0], order[1:]
    column = jnp.bitwise_xor(me, first) * width
    sliced = lax.dynamic_slice(value_states, (0, 0, column), (1, tokens, width))
    value_in = {first: [swap(sliced, first)]}
    wanted = [(first, (1,))] + [(x, (0, 1)) for x in rest]
    sent = pack_values(value_hbm, vdot_hbm, wanted, tokens, width)
    value_in[first].append(swap(sent[0], first))
    for x, array in zip(rest, sent[1:]):
        value_in[x] = [swap(array, x)]

    blocks = jnp.bitwise_xor(jnp.arange(n, dtype=jnp.int32), me.astype(jnp.int32))
    cosine, sine = rope_tables(offsets[0] + me * tokens, tokens)
    packs = rope_packs(
        blocks, queries, key_states, query_tangent, key_tangent, cosine, sine, n, sizes
    )
    packs_in = []
    for c in range(len(sizes)):
        mine = packs[c * n : (c + 1) * n]
        got = {x: swap(mine[x], x) for x in partner_order(n, "qk")}
        packs_in.append([mine[0]] + [got[x] for x in range(1, n)])
    early, late = [], []
    for c, (start, heads) in enumerate(zip(starts, sizes)):
        outs = attend(
            blocks,
            value_states,
            value_tangent,
            packs_in[c],
            [value_in[x] for x in range(1, n)],
            start,
            heads,
            n,
        )
        early.append((0, start * HD, outs[0], None))
        last = early if c < len(sizes) - 1 else late
        for x, members in routes(n, c):
            got = swap(outs[x], x, members)
            last.append((x, start * HD, got, members))
    placed = place(early, width, tokens)
    return place(late, width, tokens, placed)


def rotate(tensor, cosine, sine):
    channel = jnp.arange(tensor.shape[-1], dtype=jnp.int32)
    partner = jnp.where(
        channel % 2 == 0, -jnp.roll(tensor, -1, axis=-1), jnp.roll(tensor, 1, axis=-1)
    )
    return (tensor * cosine + partner * sine).astype(jnp.bfloat16)


def primal_terms(query_blk, keys_all, values_all, scaling):
    scores = (
        jnp.einsum("bhd,khd->hbk", query_blk, keys_all, preferred_element_type=jnp.float32)
        * scaling
    )
    largest = jnp.max(scores, axis=-1, keepdims=True)
    expons = jnp.exp(scores - largest)
    probs = expons / jnp.sum(expons, axis=-1, keepdims=True)
    weights = probs.astype(jnp.bfloat16)
    out_full = jnp.einsum("hbk,khd->bhd", weights, values_all, preferred_element_type=jnp.float32)
    return (weights, out_full)


def tangent_terms(
    query_blk, qdot_blk, keys_all, kdots_all, values_all, vdots_all, weights, out_full, scaling
):
    scores_dot = (
        jnp.einsum("bhd,khd->hbk", qdot_blk, keys_all, preferred_element_type=jnp.float32)
        + jnp.einsum("bhd,khd->hbk", query_blk, kdots_all, preferred_element_type=jnp.float32)
    ) * scaling
    product = weights.astype(jnp.float32) * scores_dot
    correction = jnp.sum(product, axis=-1)
    product_half = product.astype(jnp.bfloat16)
    tangent = (
        jnp.einsum("hbk,khd->bhd", weights, vdots_all, preferred_element_type=jnp.float32)
        + jnp.einsum("hbk,khd->bhd", product_half, values_all, preferred_element_type=jnp.float32)
        - jnp.transpose(correction)[:, :, None] * out_full
    )
    return tangent.astype(jnp.bfloat16)


def body_general(queries, key_states, value_states, query_tangent, key_tangent, value_tangent, offsets):
    devices = lax.axis_size("seq")
    repeat = max(devices // H, 1)
    per_device = max(H // devices, 1)
    groups = H // per_device
    width = per_device * HD
    tokens = queries.shape[1]
    sub_rows = tokens // repeat
    scaling = 1.0 / math.sqrt(HD)
    first = offsets[0] + lax.axis_index("seq") * tokens
    cosine, sine = (t[:, None, :] for t in rope_tables(first, tokens))

    def roped(array):
        return rotate(array[0].reshape(tokens, H, HD).astype(jnp.float32), cosine, sine).reshape(
            tokens, H * HD
        )

    def by_rows(array):
        shaped = array.reshape(repeat, sub_rows, groups, width)
        return jnp.transpose(shaped, (2, 0, 1, 3)).reshape(devices, sub_rows, width)

    def by_copies(array):
        shaped = jnp.transpose(array.reshape(tokens, groups, width), (1, 0, 2))
        spread = jnp.broadcast_to(shaped[:, None], (groups, repeat, tokens, width))
        return spread.reshape(devices, tokens, width)

    query_send = by_rows(roped(queries))
    qdot_send = by_rows(roped(query_tangent))
    key_send = by_copies(roped(key_states))
    kdot_send = by_copies(roped(key_tangent))
    value_send = by_copies(value_states[0])
    vdot_send = by_copies(value_tangent[0])
    query_rows = devices * sub_rows
    block = min(512, query_rows)
    count = query_rows // block

    def heads_view(array):
        return array.reshape(array.shape[0], per_device, HD)

    def blocks(array):
        return array.reshape(count, block, per_device, HD)

    received = (
        lax.all_to_all(query_send, "seq", split_axis=0, concat_axis=1, tiled=True),
        lax.all_to_all(key_send, "seq", split_axis=0, concat_axis=1, tiled=True),
        lax.all_to_all(value_send, "seq", split_axis=0, concat_axis=1, tiled=True),
        lax.all_to_all(qdot_send, "seq", split_axis=0, concat_axis=1, tiled=True),
        lax.all_to_all(kdot_send, "seq", split_axis=0, concat_axis=1, tiled=True),
        lax.all_to_all(vdot_send, "seq", split_axis=0, concat_axis=1, tiled=True),
    )
    query_in, key_in, value_in, qdot_in, kdot_in, vdot_in = tuple((array[0] for array in received))
    keys_all, values_all = (heads_view(key_in), heads_view(value_in))
    kdots_all, vdots_all = (heads_view(kdot_in), heads_view(vdot_in))

    def one_block(parts):
        query_blk, qdot_blk = parts
        weights, out_full = primal_terms(query_blk, keys_all, values_all, scaling)
        tangent = tangent_terms(
            query_blk,
            qdot_blk,
            keys_all,
            kdots_all,
            values_all,
            vdots_all,
            weights,
            out_full,
            scaling,
        )
        return (out_full.astype(jnp.bfloat16), tangent)

    attended, tangent_out = lax.map(one_block, (blocks(query_in), blocks(qdot_in)))

    def to_sources(array):
        return array.reshape(devices, sub_rows, width)

    returned = (
        lax.all_to_all(to_sources(attended), "seq", split_axis=0, concat_axis=0, tiled=True),
        lax.all_to_all(to_sources(tangent_out), "seq", split_axis=0, concat_axis=0, tiled=True),
    )

    def to_tokens(array):
        shaped = array.reshape(groups, repeat, sub_rows, width)
        return jnp.transpose(shaped, (1, 2, 0, 3)).reshape(tokens, H * HD)[None]

    return (to_tokens(returned[0]), to_tokens(returned[1]))


def solution(mesh):
    in_specs = (
        P(("group", "clip"), "seq", None),
        P(("group", "clip"), "seq", None),
        P(("group", "clip"), "seq", None),
        P(("group", "clip"), "seq", None),
        P(("group", "clip"), "seq", None),
        P(("group", "clip"), "seq", None),
        P(("group", "clip")),
    )
    out_specs = (P(("group", "clip"), "seq", None), P(("group", "clip"), "seq", None))
    n = mesh.shape["seq"]
    whole_heads = n > 1 and n & (n - 1) == 0 and H % n == 0
    body = body_pairs if whole_heads else body_general
    return jax.shard_map(body, mesh=mesh, in_specs=in_specs, out_specs=out_specs, check_vma=False)
```

```python
import functools
import math

import jax
import jax.numpy as jnp
from jax import lax
from jax.experimental import pallas as pl
from jax.experimental.pallas import tpu as pltpu
from jax.sharding import PartitionSpec as P


H = 16
HD = 128
HH = 44
WW = 80


rope_theta = 10000.0

SIZES = (2, 2)
ORDERS = {"v": (3, 1, 2), "qk": (2, 3, 1), "out": (3, 2, 1)}
LAST = ((3, (0, 3)), (2, None), (1, None), (3, (1, 2)))


def rope_tables(first, count):
    global_index = first + jnp.arange(count, dtype=jnp.int32)
    frames = global_index // (HH * WW)
    grid_row = global_index // WW % HH
    column = global_index % WW
    spatial = HD // 6 * 2
    temporal = HD - 2 * spatial
    channel = jnp.arange(HD, dtype=jnp.int32)
    part_start = jnp.where(
        channel < temporal, 0, jnp.where(channel < temporal + spatial, temporal, temporal + spatial)
    )
    extent = jnp.where(channel < temporal, temporal, spatial)
    pair_index = (channel - part_start) // 2
    frequency = jnp.exp(
        -(2.0 * pair_index.astype(jnp.float32) / extent.astype(jnp.float32)) * math.log(rope_theta)
    )
    position = jnp.where(
        channel[None, :] < temporal,
        frames[:, None],
        jnp.where(channel[None, :] < temporal + spatial, grid_row[:, None], column[:, None]),
    )
    angles = position.astype(jnp.float32) * frequency[None, :]
    return (jnp.cos(angles), jnp.sin(angles))


def pack_values(value, vdot, wanted, tokens, width):
    count = sum(len(arrays) for _, arrays in wanted)

    def kernel(v_ref, vdot_ref, *rest):
        outs, sems = rest[:-1], rest[-1]
        me = lax.axis_index("seq")
        copies = []
        for out, (x, arrays) in zip(outs, wanted):
            columns = pl.ds(pl.multiple_of(jnp.bitwise_xor(me, x) * width, width), width)
            for i, a in enumerate(arrays):
                copies.append(
                    pltpu.make_async_copy(
                        (v_ref, vdot_ref)[a].at[0, :, columns], out.at[i], sems.at[len(copies)]
                    )
                )
        for copy in copies:
            copy.start()
        for copy in copies:
            copy.wait()

    return pl.pallas_call(
        kernel,
        out_shape=tuple(
            jax.ShapeDtypeStruct((len(arrays), tokens, width), jnp.bfloat16)
            for _, arrays in wanted
        ),
        in_specs=[pl.BlockSpec(memory_space=pltpu.HBM)] * 2,
        out_specs=tuple(pl.BlockSpec(memory_space=pltpu.VMEM) for _ in wanted),
        scratch_shapes=[pltpu.SemaphoreType.DMA((count,))],
        compiler_params=pltpu.CompilerParams(vmem_limit_bytes=8 << 20),
        cost_estimate=pl.CostEstimate(
            flops=0, bytes_accessed=4 * count * tokens * width, transcendentals=0
        ),
        name="pack_values",
    )(value, vdot)


def rope_kernel(blk_ref, q_ref, k_ref, qd_ref, kd_ref, cos_ref, sin_ref, *outs, n, sizes):
    step = pl.program_id(0)
    cosine = cos_ref[...]
    sine = sin_ref[...]
    lane = lax.broadcasted_iota(jnp.int32, cosine.shape, 1)
    even = lane % 2 == 0
    sine_signed = jnp.where(even, -sine, sine)
    for x in range(n):

        @pl.when(step == x)
        def _(x=x):
            for a, ref in enumerate((q_ref, k_ref, qd_ref, kd_ref)):
                for c, heads in enumerate(sizes):
                    for j in range(heads):
                        at = (sum(sizes[:c]) + j) * HD
                        t = ref[0, :, at : at + HD].astype(jnp.float32)
                        partner = jnp.where(
                            even, pltpu.roll(t, HD - 1, 1), pltpu.roll(t, 1, 1)
                        )
                        y = t * cosine + partner * sine_signed
                        outs[c * n + x][a, :, j * HD : (j + 1) * HD] = y.astype(jnp.bfloat16)


def rope_packs(blocks, q, k, qd, kd, cosine, sine, n, sizes):
    tokens = q.shape[1]
    width = sum(sizes) * HD
    column = pl.BlockSpec((1, tokens, width), lambda i, blk: (0, 0, blk[i]))
    table = pl.BlockSpec((tokens, HD), lambda i, blk: (0, 0))
    shapes = [(4, tokens, heads * HD) for heads in sizes for _ in range(n)]
    return pl.pallas_call(
        functools.partial(rope_kernel, n=n, sizes=sizes),
        out_shape=tuple(jax.ShapeDtypeStruct(shape, jnp.bfloat16) for shape in shapes),
        grid_spec=pltpu.PrefetchScalarGridSpec(
            num_scalar_prefetch=1,
            grid=(n,),
            in_specs=[column] * 4 + [table] * 2,
            out_specs=tuple(pl.BlockSpec(shape, lambda i, blk: (0, 0, 0)) for shape in shapes),
        ),
        compiler_params=pltpu.CompilerParams(vmem_limit_bytes=24 << 20),
        cost_estimate=pl.CostEstimate(
            flops=4 * tokens * n * width * 6,
            bytes_accessed=16 * tokens * n * width,
            transcendentals=0,
        ),
        name="rope_packs",
    )(blocks, q, k, qd, kd, cosine, sine)


def attend_kernel(blk_ref, v_ref, vd_ref, *refs, n):
    scaling = 1.0 / math.sqrt(HD)
    packs = refs[:n]
    values = refs[n:-n]
    outs = refs[-n:]
    nt = (((1,), (1,)), ((), ()))

    def dot(a, b):
        return jnp.dot(a, b, preferred_element_type=jnp.float32)

    def dot_t(a, b):
        return lax.dot_general(a, b, nt, preferred_element_type=jnp.float32)

    keys = jnp.concatenate([p[1] for p in packs], axis=0)
    kdots = jnp.concatenate([p[3] for p in packs], axis=0)
    both = jnp.concatenate([keys, kdots], axis=1)
    rows = [v[i] for v in values for i in range(v.shape[0])]
    vals = jnp.concatenate([v_ref[0]] + rows[0::2], axis=0)
    vdots = jnp.concatenate([vd_ref[0]] + rows[1::2], axis=0)
    vboth = jnp.concatenate([vals, vdots], axis=1)
    for x in range(n):
        q = packs[x][0]
        qd = packs[x][2]
        raw = dot_t(q, keys)
        largest = jnp.max(raw, axis=-1, keepdims=True)
        expons = jnp.exp((raw - largest) * scaling)
        inverse = 1.0 / jnp.sum(expons, axis=-1, keepdims=True)
        weights = (expons * inverse).astype(jnp.bfloat16)
        scores_dot = dot_t(jnp.concatenate([qd, q], axis=1), both) * scaling
        product = weights.astype(jnp.float32) * scores_dot
        correction = jnp.sum(product, axis=-1, keepdims=True)
        mixed = dot(weights, vboth)
        out = mixed[:, :HD]
        tangent = mixed[:, HD:] + dot(product.astype(jnp.bfloat16), vals) - correction * out
        outs[x][0] = out.astype(jnp.bfloat16)
        outs[x][1] = tangent.astype(jnp.bfloat16)


def attend(blocks, value, vdot, packs, values, start, heads, n):
    tokens = value.shape[1]
    per_device = H // n
    own = pl.BlockSpec(
        (1, tokens, HD), lambda j, blk: (0, 0, blk[0] * per_device + start + j)
    )
    pack = pl.BlockSpec((4, tokens, HD), lambda j, blk: (0, 0, j))
    values = [array for arrays in values for array in arrays]
    others = [
        pl.BlockSpec((array.shape[0], tokens, HD), lambda j, blk: (0, 0, start + j))
        for array in values
    ]
    out = pl.BlockSpec((2, tokens, HD), lambda j, blk: (0, 0, j))
    pairs = (n * tokens) ** 2 * heads
    return pl.pallas_call(
        functools.partial(attend_kernel, n=n),
        out_shape=tuple(
            jax.ShapeDtypeStruct((2, tokens, heads * HD), jnp.bfloat16) for _ in range(n)
        ),
        grid_spec=pltpu.PrefetchScalarGridSpec(
            num_scalar_prefetch=1,
            grid=(heads,),
            in_specs=[own] * 2 + [pack] * n + others,
            out_specs=(out,) * n,
        ),
        compiler_params=pltpu.CompilerParams(vmem_limit_bytes=24 << 20),
        cost_estimate=pl.CostEstimate(
            flops=12 * pairs * HD,
            bytes_accessed=16 * n * tokens * heads * HD,
            transcendentals=pairs,
        ),
        name="attend",
    )(blocks, value, vdot, *packs, *values)


def place(pieces, width, tokens, into=None):
    shape = jax.ShapeDtypeStruct((1, tokens, H * HD), jnp.bfloat16)
    total = sum(piece[2].shape[2] for piece in pieces)

    def kernel(*refs):
        ins, outs, sems = refs[: len(pieces)], refs[-3:-1], refs[-1]
        me = lax.axis_index("seq")
        for act in ("start", "wait"):
            for i, (ref, (x, column, _, members)) in enumerate(zip(ins, pieces)):

                def copies(i=i, ref=ref, x=x, column=column):
                    first = pl.multiple_of(jnp.bitwise_xor(me, x) * width + column, HD)
                    for a in range(2):
                        copy = pltpu.make_async_copy(
                            ref.at[a],
                            outs[a].at[0, :, pl.ds(first, ref.shape[2])],
                            sems.at[2 * i + a],
                        )
                        getattr(copy, act)()

                if members is None:
                    copies()
                else:
                    pl.when(functools.reduce(jnp.logical_or, [me == m for m in members]))(copies)

    into = () if into is None else tuple(into)
    return pl.pallas_call(
        kernel,
        out_shape=(shape, shape),
        in_specs=[pl.BlockSpec(memory_space=pltpu.VMEM)] * len(pieces)
        + [pl.BlockSpec(memory_space=pl.ANY)] * len(into),
        out_specs=(pl.BlockSpec(memory_space=pl.ANY),) * 2,
        scratch_shapes=[pltpu.SemaphoreType.DMA((2 * len(pieces),))],
        input_output_aliases={len(pieces) + i: i for i in range(len(into))},
        compiler_params=pltpu.CompilerParams(vmem_limit_bytes=8 << 20),
        cost_estimate=pl.CostEstimate(
            flops=0, bytes_accessed=8 * tokens * total, transcendentals=0
        ),
        name="place",
    )(*(piece[2] for piece in pieces), *into)


def chunk_sizes(n):
    per_device = H // n
    return SIZES if per_device == 4 else (1,) * per_device


def routes(n, chunk):
    if n == 4 and chunk == len(chunk_sizes(n)) - 1:
        return LAST
    return [(x, None) for x in partner_order(n, "out")]


def partner_order(n, kind):
    middle_first = sorted(range(1, n), key=lambda x: (-x.bit_length(), x))
    return [x for x in ORDERS[kind] if x < n] if n == 4 else middle_first


def body_pairs(*args):
    return pairs_program(*args)


def pairs_program(queries, key_states, value_states, query_tangent, key_tangent, value_tangent, offsets):
    n = lax.axis_size("seq")
    order = partner_order(n, "v")
    sizes = chunk_sizes(n)
    starts = [sum(sizes[:c]) for c in range(len(sizes))]
    tokens = queries.shape[1]
    width = H // n * HD
    me = lax.axis_index("seq")
    value_hbm = pltpu.with_memory_space_constraint(value_states, pltpu.HBM)
    vdot_hbm = pltpu.with_memory_space_constraint(value_tangent, pltpu.HBM)

    def swap(array, x, members=None):
        pairs = [(i ^ x, i) for i in range(n) if members is None or i in members]
        return lax.ppermute(array, "seq", pairs)

    first, rest = order[0], order[1:]
    column = jnp.bitwise_xor(me, first) * width
    sliced = lax.dynamic_slice(value_states, (0, 0, column), (1, tokens, width))
    value_in = {first: [swap(sliced, first)]}
    wanted = [(first, (1,))] + [(x, (0, 1)) for x in rest]
    sent = pack_values(value_hbm, vdot_hbm, wanted, tokens, width)
    value_in[first].append(swap(sent[0], first))
    for x, array in zip(rest, sent[1:]):
        value_in[x] = [swap(array, x)]

    blocks = jnp.bitwise_xor(jnp.arange(n, dtype=jnp.int32), me.astype(jnp.int32))
    cosine, sine = rope_tables(offsets[0] + me * tokens, tokens)
    packs = rope_packs(
        blocks, queries, key_states, query_tangent, key_tangent, cosine, sine, n, sizes
    )
    packs_in = []
    for c in range(len(sizes)):
        mine = packs[c * n : (c + 1) * n]
        got = {x: swap(mine[x], x) for x in partner_order(n, "qk")}
        packs_in.append([mine[0]] + [got[x] for x in range(1, n)])
    early, late = [], []
    for c, (start, heads) in enumerate(zip(starts, sizes)):
        outs = attend(
            blocks,
            value_states,
            value_tangent,
            packs_in[c],
            [value_in[x] for x in range(1, n)],
            start,
            heads,
            n,
        )
        early.append((0, start * HD, outs[0], None))
        last = early if c < len(sizes) - 1 else late
        for x, members in routes(n, c):
            got = swap(outs[x], x, members)
            last.append((x, start * HD, got, members))
    placed = place(early, width, tokens)
    return place(late, width, tokens, placed)


def rotate(tensor, cosine, sine):
    channel = jnp.arange(tensor.shape[-1], dtype=jnp.int32)
    partner = jnp.where(
        channel % 2 == 0, -jnp.roll(tensor, -1, axis=-1), jnp.roll(tensor, 1, axis=-1)
    )
    return (tensor * cosine + partner * sine).astype(jnp.bfloat16)


def primal_terms(query_blk, keys_all, values_all, scaling):
    scores = (
        jnp.einsum("bhd,khd->hbk", query_blk, keys_all, preferred_element_type=jnp.float32)
        * scaling
    )
    largest = jnp.max(scores, axis=-1, keepdims=True)
    expons = jnp.exp(scores - largest)
    probs = expons / jnp.sum(expons, axis=-1, keepdims=True)
    weights = probs.astype(jnp.bfloat16)
    out_full = jnp.einsum("hbk,khd->bhd", weights, values_all, preferred_element_type=jnp.float32)
    return (weights, out_full)


def tangent_terms(
    query_blk, qdot_blk, keys_all, kdots_all, values_all, vdots_all, weights, out_full, scaling
):
    scores_dot = (
        jnp.einsum("bhd,khd->hbk", qdot_blk, keys_all, preferred_element_type=jnp.float32)
        + jnp.einsum("bhd,khd->hbk", query_blk, kdots_all, preferred_element_type=jnp.float32)
    ) * scaling
    product = weights.astype(jnp.float32) * scores_dot
    correction = jnp.sum(product, axis=-1)
    product_half = product.astype(jnp.bfloat16)
    tangent = (
        jnp.einsum("hbk,khd->bhd", weights, vdots_all, preferred_element_type=jnp.float32)
        + jnp.einsum("hbk,khd->bhd", product_half, values_all, preferred_element_type=jnp.float32)
        - jnp.transpose(correction)[:, :, None] * out_full
    )
    return tangent.astype(jnp.bfloat16)


def body_general(queries, key_states, value_states, query_tangent, key_tangent, value_tangent, offsets):
    devices = lax.axis_size("seq")
    repeat = max(devices // H, 1)
    per_device = max(H // devices, 1)
    groups = H // per_device
    width = per_device * HD
    tokens = queries.shape[1]
    sub_rows = tokens // repeat
    scaling = 1.0 / math.sqrt(HD)
    first = offsets[0] + lax.axis_index("seq") * tokens
    cosine, sine = (t[:, None, :] for t in rope_tables(first, tokens))

    def roped(array):
        return rotate(array[0].reshape(tokens, H, HD).astype(jnp.float32), cosine, sine).reshape(
            tokens, H * HD
        )

    def by_rows(array):
        shaped = array.reshape(repeat, sub_rows, groups, width)
        return jnp.transpose(shaped, (2, 0, 1, 3)).reshape(devices, sub_rows, width)

    def by_copies(array):
        shaped = jnp.transpose(array.reshape(tokens, groups, width), (1, 0, 2))
        spread = jnp.broadcast_to(shaped[:, None], (groups, repeat, tokens, width))
        return spread.reshape(devices, tokens, width)

    query_send = by_rows(roped(queries))
    qdot_send = by_rows(roped(query_tangent))
    key_send = by_copies(roped(key_states))
    kdot_send = by_copies(roped(key_tangent))
    value_send = by_copies(value_states[0])
    vdot_send = by_copies(value_tangent[0])
    query_rows = devices * sub_rows
    block = min(512, query_rows)
    count = query_rows // block

    def heads_view(array):
        return array.reshape(array.shape[0], per_device, HD)

    def blocks(array):
        return array.reshape(count, block, per_device, HD)

    received = (
        lax.all_to_all(query_send, "seq", split_axis=0, concat_axis=1, tiled=True),
        lax.all_to_all(key_send, "seq", split_axis=0, concat_axis=1, tiled=True),
        lax.all_to_all(value_send, "seq", split_axis=0, concat_axis=1, tiled=True),
        lax.all_to_all(qdot_send, "seq", split_axis=0, concat_axis=1, tiled=True),
        lax.all_to_all(kdot_send, "seq", split_axis=0, concat_axis=1, tiled=True),
        lax.all_to_all(vdot_send, "seq", split_axis=0, concat_axis=1, tiled=True),
    )
    query_in, key_in, value_in, qdot_in, kdot_in, vdot_in = tuple((array[0] for array in received))
    keys_all, values_all = (heads_view(key_in), heads_view(value_in))
    kdots_all, vdots_all = (heads_view(kdot_in), heads_view(vdot_in))

    def one_block(parts):
        query_blk, qdot_blk = parts
        weights, out_full = primal_terms(query_blk, keys_all, values_all, scaling)
        tangent = tangent_terms(
            query_blk,
            qdot_blk,
            keys_all,
            kdots_all,
            values_all,
            vdots_all,
            weights,
            out_full,
            scaling,
        )
        return (out_full.astype(jnp.bfloat16), tangent)

    attended, tangent_out = lax.map(one_block, (blocks(query_in), blocks(qdot_in)))

    def to_sources(array):
        return array.reshape(devices, sub_rows, width)

    returned = (
        lax.all_to_all(to_sources(attended), "seq", split_axis=0, concat_axis=0, tiled=True),
        lax.all_to_all(to_sources(tangent_out), "seq", split_axis=0, concat_axis=0, tiled=True),
    )

    def to_tokens(array):
        shaped = array.reshape(groups, repeat, sub_rows, width)
        return jnp.transpose(shaped, (1, 2, 0, 3)).reshape(tokens, H * HD)[None]

    return (to_tokens(returned[0]), to_tokens(returned[1]))


def solution(mesh):
    in_specs = (
        P(("group", "clip"), "seq", None),
        P(("group", "clip"), "seq", None),
        P(("group", "clip"), "seq", None),
        P(("group", "clip"), "seq", None),
        P(("group", "clip"), "seq", None),
        P(("group", "clip"), "seq", None),
        P(("group", "clip")),
    )
    out_specs = (P(("group", "clip"), "seq", None), P(("group", "clip"), "seq", None))
    n = mesh.shape["seq"]
    whole_heads = n > 1 and n & (n - 1) == 0 and H % n == 0
    body = body_pairs if whole_heads else body_general
    return jax.shard_map(body, mesh=mesh, in_specs=in_specs, out_specs=out_specs, check_vma=False)
```
